256 devices in a mesh: dp: 32 (over x, z), mp: 8 (over y, core).
Axes of the slice: x: 4, y: 4, z: 8, core: 2. Of those that a mesh axis runs over, the one named last changes fastest.
Arguments:
- residual_in: bfloat16 [8192, 5120], P('dp', 'mp'), may hold values from -6 to 6
- queries_in: bfloat16 [8192, 5120], P('dp', 'mp'), may hold values from -360 to 360
- key_values: bfloat16 [2, 8192, 1024], P(None, 'dp', 'mp'), may hold values from -6 to 6
- request_ids: int32 [8192], P('dp'), may hold values from 0 to 8191, as said below
- deal_order: int32 [32], replicated, may hold values from 0 to 31, each once
- page_table: int32 [512], P('dp'), may hold values from 0 to 511, as said below
- out_proj: bfloat16 [5120, 5120], P('dp', 'mp'), may hold values from -0.078125 to 0.078125
- norm_gain: bfloat16 [5120], P('mp'), may hold values from 0.099609375 to 1.8984375
- gate_up: bfloat16 [5120, 2, 16384], P('mp', None, 'dp'), may hold values from -0.078125 to 0.078125
Outputs:
- mlp_hidden: bfloat16 [8192, 16384], P('mp', 'dp')
- kv_cache: bfloat16 [512, 2, 16, 1024], P('dp', None, None, 'mp')
- residual_out: bfloat16 [8192, 5120], P('dp', 'mp')
The draws below stay inside these ranges and needn't reach their ends.
Inputs may be any that keep to these rules, and one draw needn't show every extreme that they name: `request_ids`: each request lies whole inside one aligned block of 256 packed tokens, which holds one to three requests of 32 tokens or more; its id is the index of its first token. `page_table`: each aligned block of 16 entries is a permutation of that block's own page numbers.
All inputs are finite; a program needn't handle non-finite values.
Results may differ from the reference program's by a relative error of at most 0.02.
Values may be sent and summed in bfloat16 or wider, within the bound.
No kernel may reach another device: no remote copies, remote signals or barrier semaphores. Data moves between devices by JAX's collectives and lax.ppermute only.
A program may use at most 128 MiB of HBM per device.

```python
import jax
import jax.numpy as jnp
from jax import lax

D = 5120
QH = 40
KVH = 8
HD = 128
FF = 16384
PAGE = 16
TOK_DEV = 256
TOKENS = 8192
PAGES_DEV = 16
NPAGES = 512
NBLOCKS = 32
N_MP = 8


def draw_queries_in(key, part):
    base = jnp.clip(jax.random.normal(key, (TOKENS, QH * HD), jnp.float32), -6.0, 6.0)
    return base.astype(jnp.bfloat16)


def draw_request_ids(key, part):
    places = jnp.arange(TOKENS, dtype=jnp.int32)
    block_of = places // TOK_DEV
    offset = places % TOK_DEV
    mode = jax.random.randint(jax.random.fold_in(key, 1), (NBLOCKS,), 0, 3)[block_of]
    middle = jax.random.randint(jax.random.fold_in(key, 2), (NBLOCKS,), TOK_DEV // 4, 3 * TOK_DEV // 4)[block_of]
    first_cut = jax.random.randint(jax.random.fold_in(key, 3), (NBLOCKS,), TOK_DEV // 8, 3 * TOK_DEV // 8)[block_of]
    second_cut = jax.random.randint(jax.random.fold_in(key, 4), (NBLOCKS,), 5 * TOK_DEV // 8, 7 * TOK_DEV // 8)[block_of]
    starts = (offset == 0) | (mode == 1) & (offset == middle) | (mode == 2) & ((offset == first_cut) | (offset == second_cut))
    return lax.cummax(jnp.where(starts, places, 0), axis=0).astype(jnp.int32)


def draw_page_table(key, part):
    places = jnp.arange(NPAGES, dtype=jnp.int32)
    scores = jax.random.randint(key, (NPAGES,), 0, 1 << 20) * PAGES_DEV + places % PAGES_DEV
    order = jnp.argsort(scores.reshape(-1, PAGES_DEV), axis=1, stable=True).astype(jnp.int32)
    firsts = (places // PAGES_DEV).reshape(-1, PAGES_DEV) * PAGES_DEV
    return (order + firsts).reshape(-1).astype(jnp.int32)


def block_scale(stream_key, extent, shards, low, high):
    factor_of, own = 1.0, jax.random.fold_in(stream_key, 6)
    for position, shards_of in shards:
        heights = jnp.exp(jax.random.uniform(jax.random.fold_in(own, position), (shards_of,), jnp.float32, low / len(shards), high / len(shards)))
        factor_of = factor_of * jnp.repeat(heights, extent[position] // shards_of).reshape([-1 if axis == position else 1 for axis in range(len(extent))])
    return factor_of


def centred(rng, extent, scale, limit, split=(), held_as=jnp.bfloat16):
    level = block_scale(rng, extent, split, -0.22, 0.18) if split else 1.0
    values = jax.random.normal(rng, extent, jnp.float32) * scale * level
    return jnp.minimum(jnp.maximum(values, -limit), limit).astype(held_as)


def setup_inputs(seed: int = 0) -> dict:
    arg_keys = jax.random.split(jax.random.key(seed), 10)
    residual_in = centred(arg_keys[0], (TOKENS, D), 1.0, 6.0, ((0, 32), (1, 8)))
    queries_in = draw_queries_in(jax.random.fold_in(arg_keys[9], 71), 0)
    key_values = centred(arg_keys[2], (2, TOKENS, KVH * HD), 1.0, 6.0, ((1, 32), (2, 8)))
    request_ids = draw_request_ids(jax.random.fold_in(arg_keys[9], 71), 0)
    deal_order = jax.random.permutation(arg_keys[4], NBLOCKS).astype(jnp.int32)
    page_table = draw_page_table(jax.random.fold_in(arg_keys[9], 71), 0)
    out_proj = centred(arg_keys[6], (QH * HD, D), (QH * HD) ** -0.5, 0.078125, ((0, 32), (1, 8)))
    norm_gain = jnp.clip(1.0 + 0.18 * jax.random.normal(arg_keys[7], (D,), jnp.float32), 0.099609375, 1.8984375).astype(jnp.bfloat16)
    gate_up = centred(arg_keys[8], (D, 2, FF), D ** -0.5, 0.078125, ((0, 8), (2, 32)))
    return {"residual_in": residual_in, "queries_in": queries_in, "key_values": key_values, "request_ids": request_ids, "deal_order": deal_order, "page_table": page_table, "out_proj": out_proj, "norm_gain": norm_gain, "gate_up": gate_up}


epsilon = 1e-06

def attend(queries_in, key_values, request_ids):
    tok_rows = queries_in.shape[0]
    group = QH // KVH
    queries = queries_in.astype(jnp.float32).reshape(tok_rows, KVH, group, HD)
    keys = key_values[0].astype(jnp.float32).reshape(tok_rows, KVH, HD)
    values = key_values[1].astype(jnp.float32).reshape(tok_rows, KVH, HD)
    scores = jnp.einsum('qhgd,khd->hgqk', queries, keys) * HD ** (-0.5)
    places = jnp.arange(tok_rows, dtype=jnp.int32)
    allowed = (request_ids[:, None] == request_ids[None, :]) & (places[None, :] <= places[:, None])
    scores = jnp.where(allowed, scores, -1e+30)
    row_max = lax.optimization_barrier(jnp.max(scores, axis=-1, keepdims=True))
    lifted = jnp.exp(scores - row_max)
    weights = (lifted / lax.optimization_barrier(jnp.sum(lifted, axis=-1, keepdims=True))).astype(jnp.bfloat16)
    mixed = jnp.einsum('hgqk,khd->qhgd', weights.astype(jnp.float32), values)
    return mixed.astype(jnp.bfloat16).reshape(tok_rows, QH * HD)

def reference(residual_in, queries_in, key_values, request_ids, deal_order, page_table, out_proj, norm_gain, gate_up):
    blocks = TOKENS // TOK_DEV
    q_blocks = queries_in.reshape(blocks, TOK_DEV, QH * HD)
    kv_blocks = key_values.reshape(2, blocks, TOK_DEV, KVH * HD).transpose(1, 0, 2, 3)
    id_blocks = request_ids.reshape(blocks, TOK_DEV)
    attended = lax.map(lambda item: attend(item[0], item[1], item[2]), (q_blocks, kv_blocks, id_blocks))
    attended = attended.reshape(TOKENS, QH * HD)
    projected = jnp.dot(attended, out_proj, preferred_element_type=jnp.float32)
    resid = residual_in.astype(jnp.float32) + projected
    mean_square = lax.optimization_barrier(jnp.mean(resid * resid, axis=1, keepdims=True))
    normed = (resid * lax.rsqrt(mean_square + epsilon) * norm_gain.astype(jnp.float32)).astype(jnp.bfloat16)
    arrival = jnp.take(normed.reshape(blocks, TOK_DEV, D), deal_order, axis=0).reshape(TOKENS, D)
    width = D // N_MP

    def add_share(total, index):
        columns = lax.dynamic_slice_in_dim(arrival, index * width, width, 1)
        weights = lax.dynamic_slice_in_dim(gate_up, index * width, width, 0).reshape(width, 2 * FF)
        partial_sum = jnp.dot(columns, weights, preferred_element_type=jnp.float32).astype(jnp.bfloat16)
        partial_sum = lax.optimization_barrier(partial_sum)
        return (total + partial_sum.astype(jnp.float32), None)
    summed, _ = lax.scan(add_share, jnp.zeros((TOKENS, 2 * FF), jnp.float32), jnp.arange(N_MP, dtype=jnp.int32))
    mlp_hidden = (jax.nn.silu(summed[:, :FF]) * summed[:, FF:]).astype(jnp.bfloat16)
    pages = key_values.reshape(2, NPAGES, PAGE, KVH * HD).transpose(1, 0, 2, 3)
    kv_cache = jnp.zeros_like(pages).at[page_table].set(pages)
    return (mlp_hidden, kv_cache, resid.astype(jnp.bfloat16))
```

```python
import functools

import jax
import jax.numpy as jnp
from jax import lax
from jax.experimental import pallas as pl
from jax.experimental.pallas import tpu as pltpu
from jax.sharding import PartitionSpec as P

D = 5120
HD = 128
EPS = 1e-06
NX, NZ, NY = 4, 8, 4
CHUNKS = ((32, 32), (32, 32))

BF16 = jnp.bfloat16
F32 = jnp.float32


def send_x(a, step):
    return lax.ppermute(a, "dp", [(d, (d + NZ * step) % (NX * NZ)) for d in range(NX * NZ)])


def send_z(a, step):
    return lax.ppermute(
        a, "dp", [(d, d // NZ * NZ + (d % NZ + step) % NZ) for d in range(NX * NZ)]
    )


def send_y(a, step):
    return lax.ppermute(a, "mp", [(m, (m + 2 * step) % (2 * NY)) for m in range(2 * NY)])


def swap_core(a):
    return lax.ppermute(a, "mp", [(m, m ^ 1) for m in range(2 * NY)])


def gather_x(a):
    half = a.shape[0] // 2
    up, down = send_x(a, 1), send_x(a, -1)
    far = (send_x(up[:half], 1), send_x(down[half:], -1))
    return [(a,), (down,), far, (up,)]


def gather_z(a):
    half = a.shape[0] // 2
    ups, downs = [a], [a]
    for _ in range(NZ // 2 - 1):
        ups.append(send_z(ups[-1], 1))
        downs.append(send_z(downs[-1], -1))
    far = (send_z(ups[-1][:half], 1), send_z(downs[-1][half:], -1))
    return [(a,)] + [(d,) for d in downs[1:]] + [far] + [(u,) for u in ups[:0:-1]]


def gather_xz(a):
    ring = jnp.concatenate([piece for part in gather_x(a) for piece in part], axis=0)
    ring = ring.reshape(NX, a.shape[0], a.shape[1])
    out = []
    for z, part in enumerate(gather_z(ring)):
        base = 0
        for piece in part:
            out.append((base, z, piece))
            base += piece.shape[0]
    return out


def gather_zx(b):
    ring = jnp.concatenate([piece for part in gather_z(b) for piece in part], axis=0)
    ring = ring.reshape(NZ, b.shape[0], b.shape[1])
    out = []
    for x, part in enumerate(gather_x(ring)):
        base = 0
        for piece in part:
            out.append((x, base, piece))
            base += piece.shape[0]
    return out


def attend(queries_in, key_values, request_ids):
    tok_rows = queries_in.shape[0]
    q_heads = queries_in.shape[1] // HD
    kv_heads = key_values.shape[2] // HD
    group = q_heads // kv_heads
    queries = queries_in.reshape(tok_rows, kv_heads, group, HD)
    keys = key_values[0].reshape(tok_rows, kv_heads, HD)
    values = key_values[1].reshape(tok_rows, kv_heads, HD)
    scores = jnp.einsum(
        "qhgd,khd->hgqk", queries, keys, preferred_element_type=jnp.float32
    ) * HD ** (-0.5)
    places = jnp.arange(tok_rows, dtype=jnp.int32)
    allowed = (request_ids[:, None] == request_ids[None, :]) & (places[None, :] <= places[:, None])
    scores = jnp.where(allowed, scores, -1e30)
    row_max = jnp.max(scores, axis=-1, keepdims=True)
    lifted = jnp.exp(scores - row_max)
    weights = (lifted / jnp.sum(lifted, axis=-1, keepdims=True)).astype(jnp.bfloat16)
    mixed = jnp.einsum("hgqk,khd->hgdq", weights, values, preferred_element_type=jnp.float32)
    return mixed.astype(jnp.bfloat16).reshape(q_heads * HD, tok_rows)


def project_kernel(plan, place, attended, residual, gain, *refs):
    pieces, (resid_out, keep, send, squares) = refs[: len(plan)], refs[len(plan) :]
    x, z, core = place[0], place[1], place[2]
    rows = residual.shape[0]
    total = residual[...].astype(F32)
    for (kind, x0, z0, first, count), piece in zip(plan, pieces, strict=True):
        n, depth, width = piece.shape
        parts = []
        for i in range(n):
            dx, dz = (x0 + i, z0) if kind == "xz" else (x0, z0 + i)
            owner = lax.rem(x + dx, NX) * NZ + lax.rem(z + dz, NZ)
            start = pl.multiple_of(owner * count + first, 16)
            parts.append(attended[pl.ds(start, depth), :])
        left = jnp.concatenate(parts, axis=0)
        right = piece[...].reshape(n * depth, width)
        total += lax.dot_general(left, right, (((0,), (0,)), ((), ())), preferred_element_type=F32)
    resid_out[...] = total.astype(BF16)
    squares[...] = jnp.sum(total * total, axis=1, keepdims=True)
    scaled = (total * gain[...]).astype(BF16)
    half = rows // 2
    first_half, second_half = scaled[:half], scaled[half:]
    is_first = core == 0

    @pl.when(is_first)
    def _():
        keep[...] = first_half
        send[...] = second_half

    @pl.when(jnp.logical_not(is_first))
    def _():
        keep[...] = second_half
        send[...] = first_half


def project(place, attended, residual, gain, pieces, plan):
    rows, width = residual.shape
    vmem = pl.BlockSpec(memory_space=pltpu.VMEM)
    return pl.pallas_call(
        functools.partial(project_kernel, plan),
        out_shape=(
            jax.ShapeDtypeStruct((rows, width), BF16),
            jax.ShapeDtypeStruct((rows // 2, width), BF16),
            jax.ShapeDtypeStruct((rows // 2, width), BF16),
            jax.ShapeDtypeStruct((rows, 1), F32),
        ),
        in_specs=[pl.BlockSpec(memory_space=pltpu.SMEM)] + [vmem] * (3 + len(pieces)),
        out_specs=(vmem,) * 4,
        name="project",
    )(place, attended, residual, gain, *pieces)


def partial_kernel(n_add, last, order_a, order_b, *refs):
    del order_a, order_b
    lefts, refs = refs[:8], refs[8:]
    weights, refs = refs[:2], refs[2:]
    addends, refs = refs[:n_add], refs[n_add:]
    columns = weights[0].shape[0]
    left = jnp.concatenate(
        [part for i in range(4) for part in (lefts[i][...], lefts[4 + i][...])], axis=0
    )
    total = jnp.dot(left[:, :columns], weights[0][...], preferred_element_type=F32)
    total += jnp.dot(left[:, columns:], weights[1][...], preferred_element_type=F32)
    for addend in addends:
        total += addend[...].astype(F32)
    if last:
        scale, out = refs
        half = total.shape[1] // 2
        total = total * scale[...]
        gate, up = total[:, :half], total[:, half:]
        out[...] = (gate / (1.0 + jnp.exp(-gate)) * up).astype(BF16)
    else:
        (out,) = refs
        out[...] = total.astype(BF16)


def partial_sum(order_a, order_b, left_a, left_b, weights, addends=(), scale=None):
    rows_a, depth = left_a.shape[1:]
    rows_b = left_b.shape[1]
    width = weights[0].shape[1]
    rows = 4 * (rows_a + rows_b)
    last = scale is not None

    def block_of(which, i):
        return lambda _, oa, ob: ((oa, ob)[which][i], 0, 0)

    def whole(shape):
        return pl.BlockSpec(shape, lambda _, oa, ob: (0,) * len(shape))

    in_specs = [pl.BlockSpec((None, rows_a, depth), block_of(0, i)) for i in range(4)]
    in_specs += [pl.BlockSpec((None, rows_b, depth), block_of(1, i)) for i in range(4)]
    in_specs += [whole(w.shape) for w in weights] + [whole(a.shape) for a in addends]
    args = [left_a] * 4 + [left_b] * 4 + list(weights) + list(addends)
    if last:
        in_specs.append(whole(scale.shape))
        args.append(scale)
    out_width = width // 2 if last else width
    return pl.pallas_call(
        functools.partial(partial_kernel, len(addends), last),
        out_shape=jax.ShapeDtypeStruct((rows, out_width), BF16),
        grid_spec=pltpu.PrefetchScalarGridSpec(
            num_scalar_prefetch=2,
            grid=(1,),
            in_specs=in_specs,
            out_specs=whole((rows, out_width)),
        ),
        name="last_partial" if last else "partial",
    )(order_a, order_b, *args)


def shards(
    residual_in,
    queries_in,
    key_values,
    request_ids,
    deal_order,
    page_table,
    out_proj,
    norm_gain,
    gate_up,
):
    tok_rows, local_width = residual_in.shape
    dp_index, mp_index = lax.axis_index("dp"), lax.axis_index("mp")
    x, z = dp_index // NZ, dp_index % NZ
    y, core = mp_index // 2, mp_index % 2
    hidden_here = gate_up.shape[2]

    proj_rows = out_proj.shape[0]
    proj_a = proj_rows // 2
    found_a = gather_xz(out_proj[:proj_a])
    found_b = gather_zx(out_proj[proj_a:])
    plan = [("xz", x0, z0, 0, proj_rows) for x0, z0, _ in found_a]
    plan += [("zx", x0, z0, proj_a, proj_rows) for x0, z0, _ in found_b]
    pieces = [piece for _, _, piece in found_a + found_b]

    attended = attend(queries_in, key_values, request_ids)
    all_heads = lax.all_gather(attended, "mp", axis=0, tiled=True)

    flat_weights = gate_up.reshape(local_width, 2 * hidden_here)
    weights = (flat_weights, swap_core(flat_weights))

    pages_here = page_table.shape[0]
    page_rows = tok_rows // pages_here
    channels = key_values.shape[2]
    pages = key_values.reshape(2, pages_here, page_rows, channels).transpose(1, 0, 2, 3)
    kv_cache = jnp.zeros_like(pages).at[page_table % pages_here].set(pages)

    place = jnp.stack([x, z, core]).astype(jnp.int32)
    residual_out, keep, send, squares = project(
        place,
        all_heads,
        residual_in,
        norm_gain.astype(F32).reshape(1, local_width),
        pieces,
        plan,
    )
    mine = jnp.concatenate([keep, swap_core(send)], axis=1)

    every_square = lax.all_gather(squares.reshape(tok_rows), ("dp", "mp"), axis=0, tiled=True)
    mean_square = jnp.sum(every_square.reshape(NX * NZ, 2 * NY, tok_rows), axis=1) / D
    scales = lax.rsqrt(mean_square + EPS)

    nblocks = deal_order.shape[0]
    per_chip = nblocks // NY
    arrival = (y * per_chip + jnp.arange(nblocks, dtype=jnp.int32)) % nblocks
    source = jnp.take(deal_order, arrival, mode="clip")
    dx, dz = (source // NZ - x) % NX, (source % NZ - z) % NZ
    order_a, order_b = dz * NX + dx, dx * NZ + dz
    half_rows = tok_rows // 2
    own_scales = jnp.take(scales, source[:per_chip], axis=0, mode="clip").reshape(
        per_chip, 2, half_rows
    )
    own_scales = jnp.where(core == 0, own_scales[:, 0], own_scales[:, 1])

    quads = [(order_a[4 * i : 4 * i + 4], order_b[4 * i : 4 * i + 4]) for i in range(nblocks // 4)]
    done = []
    first = 0
    for rows_a, rows_b in CHUNKS:
        rows = rows_a + rows_b
        found_a = gather_xz(mine[first : first + rows_a])
        found_b = gather_zx(mine[first + rows_a : first + rows])
        left_a = jnp.concatenate([piece for _, _, piece in found_a], axis=0)
        left_b = jnp.concatenate([piece for _, _, piece in found_b], axis=0)

        def part(i, *addends, scale=None):
            return partial_sum(*quads[i], left_a, left_b, weights, addends, scale)

        far_up = send_y(part(4), 1)
        far_down = send_y(part(5), -1)
        up_second = send_y(part(3), 1)
        down_first = send_y(part(6), -1)
        up_first = send_y(part(2, far_up), 1)
        down_second = send_y(part(7, far_down), -1)
        scale = own_scales[:, first : first + rows].reshape(2, 4 * rows, 1)
        hidden_first = part(0, up_first, down_first, scale=scale[0])
        hidden_second = part(1, up_second, down_second, scale=scale[1])
        kept = jnp.where(core == 0, hidden_first, hidden_second)
        given = swap_core(jnp.where(core == 0, hidden_second, hidden_first))
        low, high = jnp.where(core == 0, kept, given), jnp.where(core == 0, given, kept)
        done.append((low.reshape(4, rows, hidden_here), high.reshape(4, rows, hidden_here)))
        first += rows
    mlp_hidden = jnp.concatenate([low for low, _ in done] + [high for _, high in done], axis=1)
    mlp_hidden = mlp_hidden.reshape(4 * tok_rows, hidden_here)
    return (mlp_hidden, kv_cache, residual_out)


def solution(mesh):
    in_specs = (
        P("dp", "mp"),
        P("dp", "mp"),
        P(None, "dp", "mp"),
        P("dp"),
        P(),
        P("dp"),
        P("dp", "mp"),
        P("mp"),
        P("mp", None, "dp"),
    )
    out_specs = (P("mp", "dp"), P("dp", None, None, "mp"), P("dp", "mp"))
    return jax.shard_map(shards, mesh=mesh, in_specs=in_specs, out_specs=out_specs, check_vma=False)
```

```python
import functools

import jax
import jax.numpy as jnp
from jax import lax
from jax.experimental import pallas as pl
from jax.experimental.pallas import tpu as pltpu
from jax.sharding import PartitionSpec as P

D = 5120
HD = 128
EPS = 1e-06
NX, NZ, NY = 4, 8, 4
RINGS = (32, 32)

BF16 = jnp.bfloat16
F32 = jnp.float32


def send_x(a, step):
    return lax.ppermute(a, "dp", [(d, (d + NZ * step) % (NX * NZ)) for d in range(NX * NZ)])


def send_z(a, step):
    return lax.ppermute(
        a, "dp", [(d, d // NZ * NZ + (d % NZ + step) % NZ) for d in range(NX * NZ)]
    )


def send_y(a, step):
    return lax.ppermute(a, "mp", [(m, (m + 2 * step) % (2 * NY)) for m in range(2 * NY)])


def swap_core(a):
    return lax.ppermute(a, "mp", [(m, m ^ 1) for m in range(2 * NY)])


def gather_x(a):
    half = a.shape[0] // 2
    up, down = send_x(a, 1), send_x(a, -1)
    far = (send_x(up[:half], 1), send_x(down[half:], -1))
    return [(a,), (down,), far, (up,)]


def gather_z(a):
    half = a.shape[0] // 2
    ups, downs = [a], [a]
    for _ in range(NZ // 2 - 1):
        ups.append(send_z(ups[-1], 1))
        downs.append(send_z(downs[-1], -1))
    far = (send_z(ups[-1][:half], 1), send_z(downs[-1][half:], -1))
    return [(a,)] + [(d,) for d in downs[1:]] + [far] + [(u,) for u in ups[:0:-1]]


def gather_xz(a):
    ring = jnp.concatenate([piece for part in gather_x(a) for piece in part], axis=0)
    ring = ring.reshape(NX, a.shape[0], a.shape[1])
    out = []
    for z, part in enumerate(gather_z(ring)):
        base = 0
        for piece in part:
            out.append((base, z, piece))
            base += piece.shape[0]
    return out


def gather_zx(b):
    ring = jnp.concatenate([piece for part in gather_z(b) for piece in part], axis=0)
    ring = ring.reshape(NZ, b.shape[0], b.shape[1])
    out = []
    for x, part in enumerate(gather_x(ring)):
        base = 0
        for piece in part:
            out.append((x, base, piece))
            base += piece.shape[0]
    return out


def attend(queries_in, key_values, request_ids):
    tok_rows = queries_in.shape[0]
    q_heads = queries_in.shape[1] // HD
    kv_heads = key_values.shape[2] // HD
    group = q_heads // kv_heads
    queries = queries_in.reshape(tok_rows, kv_heads, group, HD)
    keys = key_values[0].reshape(tok_rows, kv_heads, HD)
    values = key_values[1].reshape(tok_rows, kv_heads, HD)
    scores = jnp.einsum(
        "qhgd,khd->hgqk", queries, keys, preferred_element_type=jnp.float32
    ) * HD ** (-0.5)
    places = jnp.arange(tok_rows, dtype=jnp.int32)
    allowed = (request_ids[:, None] == request_ids[None, :]) & (places[None, :] <= places[:, None])
    scores = jnp.where(allowed, scores, -1e30)
    row_max = jnp.max(scores, axis=-1, keepdims=True)
    lifted = jnp.exp(scores - row_max)
    weights = (lifted / jnp.sum(lifted, axis=-1, keepdims=True)).astype(jnp.bfloat16)
    mixed = jnp.einsum("hgqk,khd->hgdq", weights, values, preferred_element_type=jnp.float32)
    return mixed.astype(jnp.bfloat16).reshape(q_heads * HD, tok_rows)


def project_kernel(plan, place, attended, residual, gain, *refs):
    pieces, (resid_out, keep, send, squares) = refs[: len(plan)], refs[len(plan) :]
    x, z, core = place[0], place[1], place[2]
    rows = residual.shape[0]
    total = residual[...].astype(F32)
    for (kind, x0, z0, first, count), piece in zip(plan, pieces, strict=True):
        n, depth, width = piece.shape
        parts = []
        for i in range(n):
            dx, dz = (x0 + i, z0) if kind == "xz" else (x0, z0 + i)
            owner = lax.rem(x + dx, NX) * NZ + lax.rem(z + dz, NZ)
            start = pl.multiple_of(owner * count + first, 16)
            parts.append(attended[pl.ds(start, depth), :])
        left = jnp.concatenate(parts, axis=0)
        right = piece[...].reshape(n * depth, width)
        total += lax.dot_general(left, right, (((0,), (0,)), ((), ())), preferred_element_type=F32)
    resid_out[...] = total.astype(BF16)
    squares[...] = lax.dot_general(
        jnp.ones((8, total.shape[1]), F32),
        total * total,
        (((1,), (1,)), ((), ())),
        precision=lax.Precision.HIGHEST,
        preferred_element_type=F32,
    )
    scaled = total * gain[...]
    half = rows // 2
    first_half, second_half = scaled[:half], scaled[half:]
    is_first = core == 0

    @pl.when(is_first)
    def _():
        keep[...] = first_half
        send[...] = second_half

    @pl.when(jnp.logical_not(is_first))
    def _():
        keep[...] = second_half
        send[...] = first_half


def project(place, attended, residual, gain, pieces, plan):
    rows, width = residual.shape
    vmem = pl.BlockSpec(memory_space=pltpu.VMEM)
    return pl.pallas_call(
        functools.partial(project_kernel, plan),
        out_shape=(
            jax.ShapeDtypeStruct((rows, width), BF16),
            jax.ShapeDtypeStruct((rows // 2, width), F32),
            jax.ShapeDtypeStruct((rows // 2, width), F32),
            jax.ShapeDtypeStruct((8, rows), F32),
        ),
        in_specs=[pl.BlockSpec(memory_space=pltpu.SMEM)] + [vmem] * (3 + len(pieces)),
        out_specs=(vmem,) * 4,
        name="project",
    )(place, attended, residual, gain, *pieces)


def partial_kernel(n_left, n_add, last, *refs):
    refs = refs[n_left:]
    lefts, refs = refs[: 4 * n_left], refs[4 * n_left :]
    weights, refs = refs[0], refs[1:]
    addends, outs = refs[: 2 * n_add], refs[2 * n_add :]
    left = jnp.concatenate(
        [lefts[4 * k + i][...] for i in range(4) for k in range(n_left)], axis=0
    )
    total = jnp.dot(left, weights[...], preferred_element_type=F32)
    for quad, out in enumerate(outs):

        @pl.when(pl.program_id(0) == quad)
        def _(out=out, extra=addends[quad * n_add : (quad + 1) * n_add]):
            value = total
            for addend in extra:
                value += addend[...].astype(F32)
            if last:
                half = value.shape[1] // 2
                gate, up = value[:, :half], value[:, half:]
                value = gate / (1.0 + jnp.exp(-gate)) * up
            out[...] = value.astype(BF16)


def partial_sums(lefts, orders, weights, addends=((), ()), last=False):
    depth, width = weights.shape
    rows = 4 * sum(left.shape[1] for left in lefts)
    n_left, n_add = len(lefts), len(addends[0])

    def block_of(which, i):
        return lambda quad, *orders: (orders[which][4 * quad + i], 0, 0)

    def whole(shape):
        return pl.BlockSpec(shape, lambda quad, *orders: (0,) * len(shape))

    extra = [a for quad in addends for a in quad]
    in_specs = [
        pl.BlockSpec((None, left.shape[1], depth), block_of(k, i))
        for k, left in enumerate(lefts)
        for i in range(4)
    ]
    in_specs += [pl.BlockSpec(memory_space=pltpu.VMEM)] + [whole(a.shape) for a in extra]
    args = [left for left in lefts for _ in range(4)] + [weights] + extra
    out_shape = (rows, width // 2 if last else width)
    return pl.pallas_call(
        functools.partial(partial_kernel, n_left, n_add, last),
        out_shape=(jax.ShapeDtypeStruct(out_shape, BF16),) * 2,
        grid_spec=pltpu.PrefetchScalarGridSpec(
            num_scalar_prefetch=n_left,
            grid=(2,),
            in_specs=in_specs,
            out_specs=(whole(out_shape),) * 2,
        ),
        name="last_partials" if last else "partials",
    )(*orders, *args)


def shards(
    residual_in,
    queries_in,
    key_values,
    request_ids,
    deal_order,
    page_table,
    out_proj,
    norm_gain,
    gate_up,
):
    tok_rows, local_width = residual_in.shape
    dp_index, mp_index = lax.axis_index("dp"), lax.axis_index("mp")
    x, z = dp_index // NZ, dp_index % NZ
    y, core = mp_index // 2, mp_index % 2
    hidden_here = gate_up.shape[2]

    proj_rows = out_proj.shape[0]
    proj_a = proj_rows // 2
    found_a = gather_xz(out_proj[:proj_a])
    found_b = gather_zx(out_proj[proj_a:])
    plan = [("xz", x0, z0, 0, proj_rows) for x0, z0, _ in found_a]
    plan += [("zx", x0, z0, proj_a, proj_rows) for x0, z0, _ in found_b]
    pieces = [piece for _, _, piece in found_a + found_b]

    attended = attend(queries_in, key_values, request_ids)
    all_heads = lax.all_gather(attended, "mp", axis=0, tiled=True)

    flat_weights = gate_up.reshape(local_width, 2 * hidden_here)
    weights = jnp.concatenate([flat_weights, swap_core(flat_weights)], axis=0)

    pages_here = page_table.shape[0]
    page_rows = tok_rows // pages_here
    channels = key_values.shape[2]
    pages = key_values.reshape(2, pages_here, page_rows, channels).transpose(1, 0, 2, 3)
    kv_cache = jnp.zeros_like(pages).at[page_table % pages_here].set(pages)

    place = jnp.stack([x, z, core]).astype(jnp.int32)
    residual_out, keep, send, squares = project(
        place,
        all_heads,
        residual_in,
        norm_gain.astype(F32).reshape(1, local_width),
        pieces,
        plan,
    )
    squares = squares + swap_core(squares)
    squares = squares + send_y(squares, 1) + send_y(squares, -1) + send_y(squares, 2)
    half_rows = tok_rows // 2
    own_squares = lax.dynamic_slice_in_dim(squares[0], core * half_rows, half_rows, 0)
    scale = lax.rsqrt(own_squares / D + EPS)[:, None]
    mine = (jnp.concatenate([keep, swap_core(send)], axis=1) * scale).astype(BF16)

    nblocks = deal_order.shape[0]
    per_chip = nblocks // NY
    arrival = (y * per_chip + jnp.arange(nblocks, dtype=jnp.int32)) % nblocks
    source = jnp.take(deal_order, arrival, mode="clip")
    dx, dz = (source // NZ - x) % NX, (source % NZ - z) % NZ

    rows_a, rows_b = RINGS
    first = rows_a + rows_b
    offloaded = lax.all_gather(mine[first:], "dp", axis=0, tiled=True)
    offloaded = offloaded.reshape(nblocks, half_rows - first, 2 * local_width)
    left_a = jnp.concatenate([p for _, _, p in gather_xz(mine[:rows_a])], axis=0)
    left_b = jnp.concatenate([p for _, _, p in gather_zx(mine[rows_a:first])], axis=0)
    done = []
    for lefts, orders in (
        ((left_a, left_b), (dz * NX + dx, dx * NZ + dz)),
        ((offloaded,), (source,)),
    ):

        def part(quads, *args, **kwargs):
            picked = [jnp.concatenate([o[4 * q : 4 * q + 4] for q in quads]) for o in orders]
            return partial_sums(lefts, picked, weights, *args, **kwargs)

        far_up, far_down = part((4, 5))
        far_up, far_down = send_y(far_up, 1), send_y(far_down, -1)
        up_second, down_first = part((3, 6))
        up_second, down_first = send_y(up_second, 1), send_y(down_first, -1)
        up_first, down_second = part((2, 7), ((far_up,), (far_down,)))
        up_first, down_second = send_y(up_first, 1), send_y(down_second, -1)
        hidden_first, hidden_second = part(
            (0, 1), ((up_first, down_first), (up_second, down_second)), last=True
        )
        kept = jnp.where(core == 0, hidden_first, hidden_second)
        given = swap_core(jnp.where(core == 0, hidden_second, hidden_first))
        low, high = jnp.where(core == 0, kept, given), jnp.where(core == 0, given, kept)
        rows = kept.shape[0] // 4
        done.append((low.reshape(4, rows, hidden_here), high.reshape(4, rows, hidden_here)))
    mlp_hidden = jnp.concatenate([low for low, _ in done] + [high for _, high in done], axis=1)
    mlp_hidden = mlp_hidden.reshape(4 * tok_rows, hidden_here)
    return (mlp_hidden, kv_cache, residual_out)


def solution(mesh):
    in_specs = (
        P("dp", "mp"),
        P("dp", "mp"),
        P(None, "dp", "mp"),
        P("dp"),
        P(),
        P("dp"),
        P("dp", "mp"),
        P("mp"),
        P("mp", None, "dp"),
    )
    out_specs = (P("mp", "dp"), P("dp", None, None, "mp"), P("dp", "mp"))
    return jax.shard_map(shards, mesh=mesh, in_specs=in_specs, out_specs=out_specs, check_vma=False)
```

```python
import functools

import jax
import jax.numpy as jnp
from jax import lax
from jax.experimental import pallas as pl
from jax.experimental.pallas import tpu as pltpu
from jax.sharding import PartitionSpec as P

D = 5120
HD = 128
EPS = 1e-06
NX, NZ, NY = 4, 8, 4
ROWS_A = 32
BLOCKS = 8

BF16 = jnp.bfloat16
F32 = jnp.float32


def send_x(a, step):
    return lax.ppermute(a, "dp", [(d, (d + NZ * step) % (NX * NZ)) for d in range(NX * NZ)])


def send_z(a, step):
    return lax.ppermute(
        a, "dp", [(d, d // NZ * NZ + (d % NZ + step) % NZ) for d in range(NX * NZ)]
    )


def send_y(a, step):
    return lax.ppermute(a, "mp", [(m, (m + 2 * step) % (2 * NY)) for m in range(2 * NY)])


def swap_core(a):
    return lax.ppermute(a, "mp", [(m, m ^ 1) for m in range(2 * NY)])


def near_chip(y, core):
    return jnp.where(core == 0, y ^ 1, NY - 1 - y)


def far_chip(y, core):
    return jnp.where(core == 0, NY - 1 - y, y ^ 1)


def swap_near(a):
    return lax.ppermute(
        a, "mp", [(m, m ^ 2 if m % 2 == 0 else 2 * NY - m) for m in range(2 * NY)]
    )


def swap_far(a):
    return lax.ppermute(
        a, "mp", [(m, 2 * NY - 2 - m if m % 2 == 0 else m ^ 2) for m in range(2 * NY)]
    )


def gather_x(a):
    half = a.shape[0] // 2
    up, down = send_x(a, 1), send_x(a, -1)
    far = (send_x(up[:half], 1), send_x(down[half:], -1))
    return [(a,), (down,), far, (up,)]


def gather_z(a):
    half = a.shape[0] // 2
    ups, downs = [a], [a]
    for _ in range(NZ // 2 - 1):
        ups.append(send_z(ups[-1], 1))
        downs.append(send_z(downs[-1], -1))
    far = (send_z(ups[-1][:half], 1), send_z(downs[-1][half:], -1))
    return [(a,)] + [(d,) for d in downs[1:]] + [far] + [(u,) for u in ups[:0:-1]]


def gather_xz(a):
    ring = jnp.concatenate([piece for part in gather_x(a) for piece in part], axis=0)
    ring = ring.reshape(NX, a.shape[0], a.shape[1])
    out = []
    for z, part in enumerate(gather_z(ring)):
        base = 0
        for piece in part:
            out.append((base, z, piece))
            base += piece.shape[0]
    return out


def gather_zx(b):
    ring = jnp.concatenate([piece for part in gather_z(b) for piece in part], axis=0)
    ring = ring.reshape(NZ, b.shape[0], b.shape[1])
    out = []
    for x, part in enumerate(gather_x(ring)):
        base = 0
        for piece in part:
            out.append((x, base, piece))
            base += piece.shape[0]
    return out


def attend(queries_in, key_values, request_ids):
    tok_rows = queries_in.shape[0]
    q_heads = queries_in.shape[1] // HD
    kv_heads = key_values.shape[2] // HD
    group = q_heads // kv_heads
    queries = queries_in.reshape(tok_rows, kv_heads, group, HD)
    keys = key_values[0].reshape(tok_rows, kv_heads, HD)
    values = key_values[1].reshape(tok_rows, kv_heads, HD)
    scores = jnp.einsum(
        "qhgd,khd->hgqk", queries, keys, preferred_element_type=jnp.float32
    ) * HD ** (-0.5)
    places = jnp.arange(tok_rows, dtype=jnp.int32)
    allowed = (request_ids[:, None] == request_ids[None, :]) & (places[None, :] <= places[:, None])
    scores = jnp.where(allowed, scores, -1e30)
    row_max = jnp.max(scores, axis=-1, keepdims=True)
    lifted = jnp.exp(scores - row_max)
    weights = (lifted / jnp.sum(lifted, axis=-1, keepdims=True)).astype(jnp.bfloat16)
    mixed = jnp.einsum("hgqk,khd->hgdq", weights, values, preferred_element_type=jnp.float32)
    return mixed.astype(jnp.bfloat16).reshape(q_heads * HD, tok_rows)


def project_kernel(plan, place, attended, residual, gain, *refs):
    pieces, (resid_out, keep, send, squares) = refs[: len(plan)], refs[len(plan) :]
    x, z, core = place[0], place[1], place[2]
    rows = residual.shape[0]
    total = residual[...].astype(F32)
    for (kind, x0, z0, first, count), piece in zip(plan, pieces, strict=True):
        n, depth, width = piece.shape
        parts = []
        for i in range(n):
            dx, dz = (x0 + i, z0) if kind == "xz" else (x0, z0 + i)
            owner = lax.rem(x + dx, NX) * NZ + lax.rem(z + dz, NZ)
            start = pl.multiple_of(owner * count + first, 16)
            parts.append(attended[pl.ds(start, depth), :])
        left = jnp.concatenate(parts, axis=0)
        right = piece[...].reshape(n * depth, width)
        total += lax.dot_general(left, right, (((0,), (0,)), ((), ())), preferred_element_type=F32)
    resid_out[...] = total.astype(BF16)
    squares[...] = lax.dot_general(
        jnp.ones((8, total.shape[1]), F32),
        total * total,
        (((1,), (1,)), ((), ())),
        precision=lax.Precision.HIGHEST,
        preferred_element_type=F32,
    )
    scaled = total * gain[...]
    half = rows // 2
    first_half, second_half = scaled[:half], scaled[half:]
    is_first = core == 0

    @pl.when(is_first)
    def _():
        keep[...] = first_half
        send[...] = second_half

    @pl.when(jnp.logical_not(is_first))
    def _():
        keep[...] = second_half
        send[...] = first_half


def project(place, attended, residual, gain, pieces, plan):
    rows, width = residual.shape
    vmem = pl.BlockSpec(memory_space=pltpu.VMEM)
    return pl.pallas_call(
        functools.partial(project_kernel, plan),
        out_shape=(
            jax.ShapeDtypeStruct((rows, width), BF16),
            jax.ShapeDtypeStruct((rows // 2, width), F32),
            jax.ShapeDtypeStruct((rows // 2, width), F32),
            jax.ShapeDtypeStruct((8, rows), F32),
        ),
        in_specs=[pl.BlockSpec(memory_space=pltpu.SMEM)] + [vmem] * (3 + len(pieces)),
        out_specs=(vmem,) * 4,
        name="project",
    )(place, attended, residual, gain, *pieces)


def partial_kernel(n_add, order, *refs):
    del order
    lefts, refs = refs[:BLOCKS], refs[BLOCKS:]
    weights, addends, out = refs[0], refs[1:-1], refs[-1]
    left = jnp.concatenate([ref[...] for ref in lefts], axis=0)
    total = jnp.dot(left, weights[...], preferred_element_type=F32)
    for addend in addends:
        total += addend[...].astype(F32)
    if n_add:
        half = total.shape[1] // 2
        gate, up = total[:, :half], total[:, half:]
        total = gate / (1.0 + jnp.exp(-gate)) * up
    out[...] = total.astype(BF16)


def partial_sums(left, order, weights, addend=None):
    rows, depth = left.shape[1:]
    width = weights.shape[1]
    count = order.shape[0]
    n_add = 0 if addend is None else 1
    out_width = width // 2 if n_add else width

    def block_of(i):
        return lambda step, order: (order[BLOCKS * step + i], 0, 0)

    def stepwise(columns):
        return pl.BlockSpec((BLOCKS * rows, columns), lambda step, order: (step, 0))

    in_specs = [pl.BlockSpec((None, rows, depth), block_of(i)) for i in range(BLOCKS)]
    in_specs += [pl.BlockSpec(memory_space=pltpu.VMEM)] + [stepwise(width)] * n_add
    args = [left] * BLOCKS + [weights] + [addend] * n_add
    return pl.pallas_call(
        functools.partial(partial_kernel, n_add),
        out_shape=jax.ShapeDtypeStruct((count * rows, out_width), BF16),
        grid_spec=pltpu.PrefetchScalarGridSpec(
            num_scalar_prefetch=1,
            grid=(count // BLOCKS,),
            in_specs=in_specs,
            out_specs=stepwise(out_width),
        ),
        name="last_partials" if n_add else "partials",
    )(order, *args)


def shards(
    residual_in,
    queries_in,
    key_values,
    request_ids,
    deal_order,
    page_table,
    out_proj,
    norm_gain,
    gate_up,
):
    tok_rows, local_width = residual_in.shape
    dp_index, mp_index = lax.axis_index("dp"), lax.axis_index("mp")
    x, z = dp_index // NZ, dp_index % NZ
    y, core = mp_index // 2, mp_index % 2
    hidden_here = gate_up.shape[2]

    proj_rows = out_proj.shape[0]
    proj_a = proj_rows // 2
    found_a = gather_xz(out_proj[:proj_a])
    found_b = gather_zx(out_proj[proj_a:])
    plan = [("xz", x0, z0, 0, proj_rows) for x0, z0, _ in found_a]
    plan += [("zx", x0, z0, proj_a, proj_rows) for x0, z0, _ in found_b]
    pieces = [piece for _, _, piece in found_a + found_b]

    attended = attend(queries_in, key_values, request_ids)
    all_heads = lax.all_gather(attended, "mp", axis=0, tiled=True)

    flat_weights = gate_up.reshape(local_width, 2 * hidden_here)
    weights = jnp.concatenate([flat_weights, swap_core(flat_weights)], axis=0)
    weights = jnp.concatenate([weights, swap_near(weights)], axis=0)

    pages_here = page_table.shape[0]
    page_rows = tok_rows // pages_here
    channels = key_values.shape[2]
    pages = key_values.reshape(2, pages_here, page_rows, channels).transpose(1, 0, 2, 3)
    kv_cache = jnp.zeros_like(pages).at[page_table % pages_here].set(pages)

    place = jnp.stack([x, z, core]).astype(jnp.int32)
    place, weights = lax.optimization_barrier((place, weights))
    residual_out, keep, send, squares = project(
        place,
        all_heads,
        residual_in,
        norm_gain.astype(F32).reshape(1, local_width),
        pieces,
        plan,
    )
    squares = squares + swap_core(squares)
    squares = squares + send_y(squares, 1) + send_y(squares, -1) + send_y(squares, 2)
    quarter = tok_rows // 4
    part = jnp.where(core == 0, (y == 1) | (y == 2), y >= 2).astype(jnp.int32)
    chip = jnp.concatenate([keep, swap_core(send)], axis=1)
    mine = lax.dynamic_slice_in_dim(chip, part * quarter, quarter, 0)
    other = lax.dynamic_slice_in_dim(chip, (1 - part) * quarter, quarter, 0)
    mine = jnp.concatenate([mine, swap_near(other)], axis=1)
    own_squares = lax.dynamic_slice_in_dim(squares[0], (2 * core + part) * quarter, quarter, 0)
    mine = (mine * lax.rsqrt(own_squares / D + EPS)[:, None]).astype(BF16)

    nblocks = deal_order.shape[0]
    per_chip = nblocks // NY

    def blocks_of(first_chip):
        chips = (first_chip, near_chip(first_chip, core))
        places = [chip * per_chip + jnp.arange(per_chip, dtype=jnp.int32) for chip in chips]
        return jnp.take(deal_order, jnp.concatenate(places), mode="clip")

    theirs, ours = blocks_of(far_chip(y, core)), blocks_of(y)

    def order_a(source):
        return source % NZ * NX + (source // NZ - x) % NX

    def order_b(source):
        return (source // NZ - x) % NX * NZ + (source % NZ - z) % NZ

    ring = jnp.concatenate([p for part in gather_x(mine[:ROWS_A]) for p in part], axis=0)
    along_z = [[i * NZ + k for k in range(NZ)] for i in range(NX)]
    left_a = lax.all_gather(ring, "dp", axis=0, tiled=True, axis_index_groups=along_z)
    left_a = left_a.reshape(nblocks, ROWS_A, 4 * local_width)
    left_b = jnp.concatenate([p for _, _, p in gather_zx(mine[ROWS_A:])], axis=0)
    left_b = left_b.reshape(nblocks, quarter - ROWS_A, 4 * local_width)

    done = []
    for left, order in ((left_b, order_b), (left_a, order_a)):
        rows = left.shape[1]
        found = swap_far(partial_sums(left, order(theirs), weights))
        hidden = partial_sums(left, order(ours), weights, found)
        hidden = hidden.reshape(2, 2, 4, rows, hidden_here)
        kept, given = hidden[0], swap_near(hidden[1])
        low, high = jnp.where(part == 0, kept, given), jnp.where(part == 0, given, kept)
        both = jnp.stack([low, high], axis=1)
        own = jnp.where(core == 0, both[0], both[1])
        got = swap_core(jnp.where(core == 0, both[1], both[0]))
        halves = jnp.stack([jnp.where(core == 0, own, got), jnp.where(core == 0, got, own)])
        done.append(halves.transpose(2, 0, 1, 3, 4))
    mlp_hidden = jnp.concatenate(done[::-1], axis=3).reshape(4 * tok_rows, hidden_here)
    return (mlp_hidden, kv_cache, residual_out)


def solution(mesh):
    in_specs = (
        P("dp", "mp"),
        P("dp", "mp"),
        P(None, "dp", "mp"),
        P("dp"),
        P(),
        P("dp"),
        P("dp", "mp"),
        P("mp"),
        P("mp", None, "dp"),
    )
    out_specs = (P("mp", "dp"), P("dp", None, None, "mp"), P("dp", "mp"))
    return jax.shard_map(shards, mesh=mesh, in_specs=in_specs, out_specs=out_specs, check_vma=False)
```

```python
import functools

import jax
import jax.numpy as jnp
from jax import lax
from jax.experimental import pallas as pl
from jax.experimental.pallas import tpu as pltpu
from jax.sharding import PartitionSpec as P

D = 5120
HD = 128
EPS = 1e-06
NX, NZ, NY = 4, 8, 4
ROWS_A = 32
BLOCKS = 8

BF16 = jnp.bfloat16
F32 = jnp.float32


def send_x(a, step):
    return lax.ppermute(a, "dp", [(d, (d + NZ * step) % (NX * NZ)) for d in range(NX * NZ)])


def send_z(a, step):
    return lax.ppermute(
        a, "dp", [(d, d // NZ * NZ + (d % NZ + step) % NZ) for d in range(NX * NZ)]
    )


def send_y(a, step):
    return lax.ppermute(a, "mp", [(m, (m + 2 * step) % (2 * NY)) for m in range(2 * NY)])


def swap_core(a):
    return lax.ppermute(a, "mp", [(m, m ^ 1) for m in range(2 * NY)])


def near_chip(y, core):
    return jnp.where(core == 0, y ^ 1, NY - 1 - y)


def far_chip(y, core):
    return jnp.where(core == 0, NY - 1 - y, y ^ 1)


def part_of(y, core):
    return jnp.where(core == 0, (y == 1) | (y == 2), y >= 2).astype(jnp.int32)


def swap_near(a):
    return lax.ppermute(
        a, "mp", [(m, m ^ 2 if m % 2 == 0 else 2 * NY - m) for m in range(2 * NY)]
    )


def swap_far(a):
    return lax.ppermute(
        a, "mp", [(m, 2 * NY - 2 - m if m % 2 == 0 else m ^ 2) for m in range(2 * NY)]
    )


def swap_both(a):
    return lax.ppermute(
        a, "mp", [(m, (m ^ 2) + 1 if m % 2 == 0 else 2 * NY - 1 - m) for m in range(2 * NY)]
    )


def gather_x(a):
    half = a.shape[0] // 2
    up, down = send_x(a, 1), send_x(a, -1)
    far = (send_x(up[:half], 1), send_x(down[half:], -1))
    return [(a,), (down,), far, (up,)]


def offload_z(a):
    groups = [[i * NZ + k for k in range(NZ)] for i in range(NX)]
    return lax.all_gather(a, "dp", axis=0, tiled=True, axis_index_groups=groups)


def gather_dp(a, b):
    ring_b = offload_z(b)
    ring_a = jnp.concatenate([p for part in gather_x(a) for p in part], axis=0)
    ring_a, ring_b = lax.optimization_barrier((ring_a, ring_b))
    found_a = offload_z(ring_a).reshape(NX * NZ, *a.shape)
    found_b = []
    for offset, part in enumerate(gather_x(ring_b.reshape(NZ, *b.shape))):
        base = 0
        for piece in part:
            found_b.append((offset, base, piece))
            base += piece.shape[0]
    return found_a, found_b


def gather_heads(a):
    half = a.shape[0] // 2
    up, down = send_y(a, 1), send_y(a, -1)
    mine = jnp.concatenate([a, down, send_y(up[:half], 1), send_y(down[half:], -1), up], axis=0)
    return jnp.concatenate([mine, swap_core(mine)], axis=0)


def attend(queries_in, key_values, request_ids):
    tok_rows = queries_in.shape[0]
    q_heads = queries_in.shape[1] // HD
    kv_heads = key_values.shape[2] // HD
    group = q_heads // kv_heads
    queries = queries_in.reshape(tok_rows, kv_heads, group, HD)
    keys = key_values[0].reshape(tok_rows, kv_heads, HD)
    values = key_values[1].reshape(tok_rows, kv_heads, HD)
    scores = jnp.einsum(
        "qhgd,khd->hgqk", queries, keys, preferred_element_type=jnp.float32
    ) * HD ** (-0.5)
    places = jnp.arange(tok_rows, dtype=jnp.int32)
    allowed = (request_ids[:, None] == request_ids[None, :]) & (places[None, :] <= places[:, None])
    scores = jnp.where(allowed, scores, -1e30)
    row_max = jnp.max(scores, axis=-1, keepdims=True)
    lifted = jnp.exp(scores - row_max)
    weights = (lifted / jnp.sum(lifted, axis=-1, keepdims=True)).astype(jnp.bfloat16)
    mixed = jnp.einsum("hgqk,khd->hgdq", weights, values, preferred_element_type=jnp.float32)
    return mixed.astype(jnp.bfloat16).reshape(q_heads * HD, tok_rows)


def product(place, attended, piece, plan, first, count):
    x, y, core = place[0], place[1], place[2]
    n, depth, width = piece.shape
    heads = attended.shape[0] // (2 * NY)
    per_device = heads // count
    total = None
    for low in range(0, n, BLOCKS):
        parts = []
        for dx, z in plan[low : low + BLOCKS]:
            owner = lax.rem(x + dx, NX) * NZ + z
            m = owner // per_device
            where = jnp.bitwise_xor(lax.rem(m, 2), core) * NY + lax.rem(m // 2 - y + NY, NY)
            start = where * heads + lax.rem(owner, per_device) * count + first
            parts.append(attended[pl.ds(pl.multiple_of(start, 16), depth), :])
        left = jnp.concatenate(parts, axis=0)
        right = piece[low : low + len(parts)].reshape(len(parts) * depth, width)
        term = lax.dot_general(left, right, (((0,), (0,)), ((), ())), preferred_element_type=F32)
        total = term if total is None else total + term
    return total


def project_b_kernel(plans, first, count, place, attended, residual, *refs):
    pieces, out = refs[:-1], refs[-1]
    total = residual[...].astype(F32)
    for plan, piece in zip(plans, pieces, strict=True):
        total += product(place, attended, piece, plan, first, count)
    out[...] = total


def project_b(place, attended, residual, found, first, count):
    vmem = pl.BlockSpec(memory_space=pltpu.VMEM)
    plans = [[(dx, z0 + i) for i in range(p.shape[0])] for dx, z0, p in found]
    return pl.pallas_call(
        functools.partial(project_b_kernel, plans, first, count),
        out_shape=jax.ShapeDtypeStruct(residual.shape, F32),
        in_specs=[pl.BlockSpec(memory_space=pltpu.SMEM)] + [vmem] * (2 + len(found)),
        out_specs=vmem,
        name="project_b",
    )(place, attended, residual, *[p for _, _, p in found])


def project_a_kernel(count, place, attended, so_far, gain, piece, resid_out, keep, send, squares):
    rows = so_far.shape[0]
    plan = [(dx, z) for z in range(NZ) for dx in range(NX)]
    total = so_far[...] + product(place, attended, piece, plan, 0, count)
    resid_out[...] = total.astype(BF16)
    squares[...] = lax.dot_general(
        jnp.ones((8, total.shape[1]), F32),
        total * total,
        (((1,), (1,)), ((), ())),
        precision=lax.Precision.HIGHEST,
        preferred_element_type=F32,
    )
    scaled = total * gain[...]
    half = rows // 2
    first_half, second_half = scaled[:half], scaled[half:]
    is_first = place[2] == 0

    @pl.when(is_first)
    def _():
        keep[...] = first_half
        send[...] = second_half

    @pl.when(jnp.logical_not(is_first))
    def _():
        keep[...] = second_half
        send[...] = first_half


def project_a(place, attended, so_far, gain, piece, count):
    rows, width = so_far.shape
    vmem = pl.BlockSpec(memory_space=pltpu.VMEM)
    return pl.pallas_call(
        functools.partial(project_a_kernel, count),
        out_shape=(
            jax.ShapeDtypeStruct((rows, width), BF16),
            jax.ShapeDtypeStruct((rows // 2, width), F32),
            jax.ShapeDtypeStruct((rows // 2, width), F32),
            jax.ShapeDtypeStruct((8, rows), F32),
        ),
        in_specs=[pl.BlockSpec(memory_space=pltpu.SMEM)] + [vmem] * 4,
        out_specs=(vmem,) * 4,
        name="project_a",
    )(place, attended, so_far, gain, piece)


def partial_kernel(n_add, order, *refs):
    del order
    lefts, refs = refs[:BLOCKS], refs[BLOCKS:]
    weights, addends, out = refs[:2], refs[2:-1], refs[-1]
    left = jnp.concatenate([ref[...] for ref in lefts], axis=0)
    depth = weights[0].shape[0]
    total = jnp.dot(left[:, :depth], weights[0][...], preferred_element_type=F32)
    total += jnp.dot(left[:, depth:], weights[1][...], preferred_element_type=F32)
    for addend in addends:
        total += addend[...].astype(F32)
    if n_add:
        half = total.shape[1] // 2
        gate, up = total[:, :half], total[:, half:]
        total = gate / (1.0 + jnp.exp(-gate)) * up
    out[...] = total.astype(BF16)


def partial_sums(left, order, weights, addend=None):
    rows, depth = left.shape[1:]
    width = weights[0].shape[1]
    count = order.shape[0]
    n_add = 0 if addend is None else 1
    out_width = width // 2 if n_add else width

    def block_of(i):
        return lambda step, order: (order[BLOCKS * step + i], 0, 0)

    def stepwise(columns):
        return pl.BlockSpec((BLOCKS * rows, columns), lambda step, order: (step, 0))

    in_specs = [pl.BlockSpec((None, rows, depth), block_of(i)) for i in range(BLOCKS)]
    in_specs += [pl.BlockSpec(memory_space=pltpu.VMEM)] * 2 + [stepwise(width)] * n_add
    args = [left] * BLOCKS + list(weights) + [addend] * n_add
    return pl.pallas_call(
        functools.partial(partial_kernel, n_add),
        out_shape=jax.ShapeDtypeStruct((count * rows, out_width), BF16),
        grid_spec=pltpu.PrefetchScalarGridSpec(
            num_scalar_prefetch=1,
            grid=(count // BLOCKS,),
            in_specs=in_specs,
            out_specs=stepwise(out_width),
        ),
        compiler_params=pltpu.CompilerParams(vmem_limit_bytes=32 * 2**20),
        name="last_partials" if n_add else "partials",
    )(order, *args)


def shards(
    residual_in,
    queries_in,
    key_values,
    request_ids,
    deal_order,
    page_table,
    out_proj,
    norm_gain,
    gate_up,
):
    tok_rows, local_width = residual_in.shape
    dp_index, mp_index = lax.axis_index("dp"), lax.axis_index("mp")
    x, z = dp_index // NZ, dp_index % NZ
    y, core = mp_index // 2, mp_index % 2
    hidden_here = gate_up.shape[2]

    count = out_proj.shape[0]
    first_b = count // 2
    found_a, found_b = gather_dp(out_proj[:first_b], out_proj[first_b:])
    all_heads = gather_heads(attend(queries_in, key_values, request_ids))

    flat_weights = gate_up.reshape(local_width, 2 * hidden_here)
    chip_weights = jnp.concatenate([flat_weights, swap_core(flat_weights)], axis=0)
    all_heads, chip_weights = lax.optimization_barrier((all_heads, chip_weights))
    weights = (chip_weights, swap_near(chip_weights))

    pages_here = page_table.shape[0]
    page_rows = tok_rows // pages_here
    channels = key_values.shape[2]
    pages = key_values.reshape(2, pages_here, page_rows, channels).transpose(1, 0, 2, 3)
    kv_cache = jnp.zeros_like(pages).at[page_table % pages_here].set(pages)

    place = jnp.stack([x, y, core]).astype(jnp.int32)
    so_far = project_b(place, all_heads, residual_in, found_b, first_b, count)
    gain = norm_gain.astype(F32).reshape(1, local_width)
    so_far, weights = lax.optimization_barrier((so_far, weights))
    residual_out, keep, send, squares = project_a(place, all_heads, so_far, gain, found_a, count)
    squares = squares + swap_core(squares)
    squares = squares + send_y(squares, 1) + send_y(squares, -1) + send_y(squares, 2)
    quarter = tok_rows // 4
    part = part_of(y, core)
    chip = jnp.concatenate([keep, swap_core(send)], axis=1)
    mine = lax.dynamic_slice_in_dim(chip, part * quarter, quarter, 0)
    other = lax.dynamic_slice_in_dim(chip, (1 - part) * quarter, quarter, 0)
    mine = jnp.concatenate([mine, swap_near(other)], axis=1)
    own_squares = lax.dynamic_slice_in_dim(squares[0], (2 * core + part) * quarter, quarter, 0)
    mine = (mine * lax.rsqrt(own_squares / D + EPS)[:, None]).astype(BF16)

    nblocks = deal_order.shape[0]
    per_chip = nblocks // NY

    def blocks_of(first_chip):
        places = [
            (chip * 2 + which) * 4 + jnp.arange(4, dtype=jnp.int32)
            for chip in (first_chip, near_chip(first_chip, core))
            for which in (core, 1 - core)
        ]
        return jnp.take(deal_order, jnp.concatenate(places), mode="clip")

    theirs, ours = blocks_of(far_chip(y, core)), blocks_of(y)
    left_a, found_b = gather_dp(mine[:ROWS_A], mine[ROWS_A:])
    left_b = jnp.concatenate([piece for _, _, piece in found_b], axis=0)

    other_part = part_of(y, 1 - core)
    quarters = (
        2 * core + part,
        2 * (1 - core) + other_part,
        2 * core + 1 - part,
        2 * (1 - core) + 1 - other_part,
    )
    mlp_hidden = jnp.zeros((4, 4, quarter, hidden_here), BF16)
    for left, first, order_of in (
        (left_b, ROWS_A, lambda s: (s // NZ - x) % NX * NZ + s % NZ),
        (left_a, 0, lambda s: s % NZ * NX + (s // NZ - x) % NX),
    ):
        rows = left.shape[1]
        found = swap_far(partial_sums(left, order_of(theirs), weights))
        hidden = partial_sums(left, order_of(ours), weights, found)
        hidden = hidden.reshape(4, 4, 1, rows, hidden_here)
        parts = (hidden[0], swap_core(hidden[1]), swap_near(hidden[2]), swap_both(hidden[3]))
        for which, value in zip(quarters, parts, strict=True):
            mlp_hidden = lax.dynamic_update_slice(mlp_hidden, value, (0, which, first, 0))
    mlp_hidden = mlp_hidden.reshape(4 * tok_rows, hidden_here)
    return (mlp_hidden, kv_cache, residual_out)


def solution(mesh):
    in_specs = (
        P("dp", "mp"),
        P("dp", "mp"),
        P(None, "dp", "mp"),
        P("dp"),
        P(),
        P("dp"),
        P("dp", "mp"),
        P("mp"),
        P("mp", None, "dp"),
    )
    out_specs = (P("mp", "dp"), P("dp", None, None, "mp"), P("dp", "mp"))
    return jax.shard_map(shards, mesh=mesh, in_specs=in_specs, out_specs=out_specs, check_vma=False)
```

```python
import functools

import jax
import jax.numpy as jnp
from jax import lax
from jax.experimental import pallas as pl
from jax.experimental.pallas import tpu as pltpu
from jax.sharding import PartitionSpec as P

D = 5120
HD = 128
EPS = 1e-06
NX, NZ, NY = 4, 8, 4
ROWS_A = 32
BLOCKS = 8

BF16 = jnp.bfloat16
F32 = jnp.float32


def send_x(a, step):
    return lax.ppermute(a, "dp", [(d, (d + NZ * step) % (NX * NZ)) for d in range(NX * NZ)])


def send_z(a, step):
    return lax.ppermute(
        a, "dp", [(d, d // NZ * NZ + (d % NZ + step) % NZ) for d in range(NX * NZ)]
    )


def send_y(a, step):
    return lax.ppermute(a, "mp", [(m, (m + 2 * step) % (2 * NY)) for m in range(2 * NY)])


def swap_core(a):
    return lax.ppermute(a, "mp", [(m, m ^ 1) for m in range(2 * NY)])


def near_chip(y, core):
    return jnp.where(core == 0, y ^ 1, NY - 1 - y)


def far_chip(y, core):
    return jnp.where(core == 0, NY - 1 - y, y ^ 1)


def part_of(y, core):
    return jnp.where(core == 0, (y == 1) | (y == 2), y >= 2).astype(jnp.int32)


def swap_near(a):
    return lax.ppermute(
        a, "mp", [(m, m ^ 2 if m % 2 == 0 else 2 * NY - m) for m in range(2 * NY)]
    )


def swap_far(a):
    return lax.ppermute(
        a, "mp", [(m, 2 * NY - 2 - m if m % 2 == 0 else m ^ 2) for m in range(2 * NY)]
    )


def swap_both(a):
    return lax.ppermute(
        a, "mp", [(m, (m ^ 2) + 1 if m % 2 == 0 else 2 * NY - 1 - m) for m in range(2 * NY)]
    )


def gather_x(a):
    half = a.shape[0] // 2
    up, down = send_x(a, 1), send_x(a, -1)
    far = (send_x(up[:half], 1), send_x(down[half:], -1))
    return [(a,), (down,), far, (up,)]


def offload_z(a):
    groups = [[i * NZ + k for k in range(NZ)] for i in range(NX)]
    return lax.all_gather(a, "dp", axis=0, tiled=True, axis_index_groups=groups)


def gather_z(a):
    half = a.shape[0] // 2
    ups, downs = [a], [a]
    for _ in range(NZ // 2 - 1):
        ups.append(send_z(ups[-1], 1))
        downs.append(send_z(downs[-1], -1))
    far = (send_z(ups[-1][:half], 1), send_z(downs[-1][half:], -1))
    return [(a,)] + [(d,) for d in downs[1:]] + [far] + [(u,) for u in ups[:0:-1]]


def gather_xz(a):
    ring = jnp.concatenate([piece for part in gather_x(a) for piece in part], axis=0)
    ring = ring.reshape(NX, a.shape[0], a.shape[1])
    out = []
    for z, part in enumerate(gather_z(ring)):
        base = 0
        for piece in part:
            out.append((base, z, piece))
            base += piece.shape[0]
    return out


def gather_zx(b):
    ring = jnp.concatenate([piece for part in gather_z(b) for piece in part], axis=0)
    ring = ring.reshape(NZ, b.shape[0], b.shape[1])
    out = []
    for x, part in enumerate(gather_x(ring)):
        base = 0
        for piece in part:
            out.append((x, base, piece))
            base += piece.shape[0]
    return out


def gather_dp(a, b):
    half_a, half_b = a.shape[0] // 2, b.shape[0] // 2
    up_x, down_x, up_z, down_z = lax.optimization_barrier(
        (send_x(a, 1), send_x(a, -1), send_z(b, 1), send_z(b, -1))
    )
    far_x = (send_x(up_x[:half_a], 1), send_x(down_x[half_a:], -1))
    far_x, up_2, down_2 = lax.optimization_barrier((far_x, send_z(up_z, 1), send_z(down_z, -1)))
    ring_a = jnp.concatenate([a, down_x, *far_x, up_x], axis=0)
    found_a = offload_z(ring_a).reshape(NX * NZ, *a.shape)
    up_3, down_3 = send_z(up_2, 1), send_z(down_2, -1)
    far_z = (send_z(up_3[:half_b], 1), send_z(down_3[half_b:], -1))
    ring_b = [b, down_z, down_2, down_3, *far_z, up_3, up_2, up_z]
    ring_b = jnp.concatenate(ring_b, axis=0).reshape(NZ, *b.shape)
    found_b = jnp.concatenate([p for part in gather_x(ring_b) for p in part], axis=0)
    return found_a, found_b


def attend(queries_in, key_values, request_ids):
    tok_rows = queries_in.shape[0]
    q_heads = queries_in.shape[1] // HD
    kv_heads = key_values.shape[2] // HD
    group = q_heads // kv_heads
    queries = queries_in.reshape(tok_rows, kv_heads, group, HD)
    keys = key_values[0].reshape(tok_rows, kv_heads, HD)
    values = key_values[1].reshape(tok_rows, kv_heads, HD)
    scores = jnp.einsum(
        "qhgd,khd->hgqk", queries, keys, preferred_element_type=jnp.float32
    ) * HD ** (-0.5)
    places = jnp.arange(tok_rows, dtype=jnp.int32)
    allowed = (request_ids[:, None] == request_ids[None, :]) & (places[None, :] <= places[:, None])
    scores = jnp.where(allowed, scores, -1e30)
    row_max = jnp.max(scores, axis=-1, keepdims=True)
    lifted = jnp.exp(scores - row_max)
    weights = (lifted / jnp.sum(lifted, axis=-1, keepdims=True)).astype(jnp.bfloat16)
    mixed = jnp.einsum("hgqk,khd->hgdq", weights, values, preferred_element_type=jnp.float32)
    return mixed.astype(jnp.bfloat16).reshape(q_heads * HD, tok_rows)


def project_kernel(plan, place, attended, residual, gain, *refs):
    pieces, (resid_out, keep, send, squares) = refs[: len(plan)], refs[len(plan) :]
    x, z, core = place[0], place[1], place[2]
    rows = residual.shape[0]
    total = residual[...].astype(F32)
    for (kind, x0, z0, first, count), piece in zip(plan, pieces, strict=True):
        n, depth, width = piece.shape
        parts = []
        for i in range(n):
            dx, dz = (x0 + i, z0) if kind == "xz" else (x0, z0 + i)
            owner = lax.rem(x + dx, NX) * NZ + lax.rem(z + dz, NZ)
            start = pl.multiple_of(owner * count + first, 16)
            parts.append(attended[pl.ds(start, depth), :])
        left = jnp.concatenate(parts, axis=0)
        right = piece[...].reshape(n * depth, width)
        total += lax.dot_general(left, right, (((0,), (0,)), ((), ())), preferred_element_type=F32)
    resid_out[...] = total.astype(BF16)
    squares[...] = lax.dot_general(
        jnp.ones((8, total.shape[1]), F32),
        total * total,
        (((1,), (1,)), ((), ())),
        precision=lax.Precision.HIGHEST,
        preferred_element_type=F32,
    )
    scaled = total * gain[...]
    half = rows // 2
    first_half, second_half = scaled[:half], scaled[half:]
    is_first = core == 0

    @pl.when(is_first)
    def _():
        keep[...] = first_half
        send[...] = second_half

    @pl.when(jnp.logical_not(is_first))
    def _():
        keep[...] = second_half
        send[...] = first_half


def project(place, attended, residual, gain, pieces, plan):
    rows, width = residual.shape
    vmem = pl.BlockSpec(memory_space=pltpu.VMEM)
    return pl.pallas_call(
        functools.partial(project_kernel, plan),
        out_shape=(
            jax.ShapeDtypeStruct((rows, width), BF16),
            jax.ShapeDtypeStruct((rows // 2, width), F32),
            jax.ShapeDtypeStruct((rows // 2, width), F32),
            jax.ShapeDtypeStruct((8, rows), F32),
        ),
        in_specs=[pl.BlockSpec(memory_space=pltpu.SMEM)] + [vmem] * (3 + len(pieces)),
        out_specs=(vmem,) * 4,
        name="project",
    )(place, attended, residual, gain, *pieces)


def partial_kernel(n_add, order, *refs):
    del order
    lefts, refs = refs[:BLOCKS], refs[BLOCKS:]
    weights, addends, out = refs[:2], refs[2:-1], refs[-1]
    left = jnp.concatenate([ref[...] for ref in lefts], axis=0)
    depth = weights[0].shape[0]
    total = jnp.dot(left[:, :depth], weights[0][...], preferred_element_type=F32)
    total += jnp.dot(left[:, depth:], weights[1][...], preferred_element_type=F32)
    for addend in addends:
        total += addend[...].astype(F32)
    if n_add:
        half = total.shape[1] // 2
        gate, up = total[:, :half], total[:, half:]
        total = gate / (1.0 + jnp.exp(-gate)) * up
    out[...] = total.astype(BF16)


def partial_sums(left, order, weights, addend=None):
    rows, depth = left.shape[1:]
    width = weights[0].shape[1]
    count = order.shape[0]
    n_add = 0 if addend is None else 1
    out_width = width // 2 if n_add else width

    def block_of(i):
        return lambda step, order: (order[BLOCKS * step + i], 0, 0)

    def stepwise(columns):
        return pl.BlockSpec((BLOCKS * rows, columns), lambda step, order: (step, 0))

    in_specs = [pl.BlockSpec((None, rows, depth), block_of(i)) for i in range(BLOCKS)]
    in_specs += [pl.BlockSpec(memory_space=pltpu.VMEM)] * 2 + [stepwise(width)] * n_add
    args = [left] * BLOCKS + list(weights) + [addend] * n_add
    return pl.pallas_call(
        functools.partial(partial_kernel, n_add),
        out_shape=jax.ShapeDtypeStruct((count * rows, out_width), BF16),
        grid_spec=pltpu.PrefetchScalarGridSpec(
            num_scalar_prefetch=1,
            grid=(count // BLOCKS,),
            in_specs=in_specs,
            out_specs=stepwise(out_width),
        ),
        compiler_params=pltpu.CompilerParams(vmem_limit_bytes=56 * 2**20),
        name="last_partials" if n_add else "partials",
    )(order, *args)


def shards(
    residual_in,
    queries_in,
    key_values,
    request_ids,
    deal_order,
    page_table,
    out_proj,
    norm_gain,
    gate_up,
):
    tok_rows, local_width = residual_in.shape
    dp_index, mp_index = lax.axis_index("dp"), lax.axis_index("mp")
    x, z = dp_index // NZ, dp_index % NZ
    y, core = mp_index // 2, mp_index % 2
    hidden_here = gate_up.shape[2]

    proj_rows = out_proj.shape[0]
    proj_a = proj_rows // 2
    found_a = gather_xz(out_proj[:proj_a])
    found_b = gather_zx(out_proj[proj_a:])
    plan = [("xz", x0, z0, 0, proj_rows) for x0, z0, _ in found_a]
    plan += [("zx", x0, z0, proj_a, proj_rows) for x0, z0, _ in found_b]
    pieces = [piece for _, _, piece in found_a + found_b]

    attended = attend(queries_in, key_values, request_ids)
    all_heads = lax.all_gather(attended, "mp", axis=0, tiled=True)

    flat_weights = gate_up.reshape(local_width, 2 * hidden_here)
    chip_weights = jnp.concatenate([flat_weights, swap_core(flat_weights)], axis=0)
    weights = (chip_weights, swap_near(chip_weights))

    pages_here = page_table.shape[0]
    page_rows = tok_rows // pages_here
    channels = key_values.shape[2]
    pages = key_values.reshape(2, pages_here, page_rows, channels).transpose(1, 0, 2, 3)
    kv_cache = jnp.zeros_like(pages).at[page_table % pages_here].set(pages)

    place = jnp.stack([x, z, core]).astype(jnp.int32)
    place, weights = lax.optimization_barrier((place, weights))
    residual_out, keep, send, squares = project(
        place,
        all_heads,
        residual_in,
        norm_gain.astype(F32).reshape(1, local_width),
        pieces,
        plan,
    )
    squares = squares + swap_core(squares)
    squares = squares + send_y(squares, 1) + send_y(squares, -1) + send_y(squares, 2)
    quarter = tok_rows // 4
    part = part_of(y, core)
    chip = jnp.concatenate([keep, swap_core(send)], axis=1)
    mine = lax.dynamic_slice_in_dim(chip, part * quarter, quarter, 0)
    other = lax.dynamic_slice_in_dim(chip, (1 - part) * quarter, quarter, 0)
    mine = jnp.concatenate([mine, swap_near(other)], axis=1)
    own_squares = lax.dynamic_slice_in_dim(squares[0], (2 * core + part) * quarter, quarter, 0)
    mine = (mine * lax.rsqrt(own_squares / D + EPS)[:, None]).astype(BF16)

    nblocks = deal_order.shape[0]
    per_chip = nblocks // NY

    def blocks_of(first_chip):
        places = [
            (chip * 2 + which) * 4 + jnp.arange(4, dtype=jnp.int32)
            for chip in (first_chip, near_chip(first_chip, core))
            for which in (core, 1 - core)
        ]
        return jnp.take(deal_order, jnp.concatenate(places), mode="clip")

    theirs, ours = blocks_of(far_chip(y, core)), blocks_of(y)
    left_a, left_b = gather_dp(mine[:ROWS_A], mine[ROWS_A:])

    other_part = part_of(y, 1 - core)
    quarters = (
        2 * core + part,
        2 * (1 - core) + other_part,
        2 * core + 1 - part,
        2 * (1 - core) + 1 - other_part,
    )
    mlp_hidden = jnp.zeros((4, 4, quarter, hidden_here), BF16)
    for left, first, order_of in (
        (left_b, ROWS_A, lambda s: (s // NZ - x) % NX * NZ + (s % NZ - z) % NZ),
        (left_a, 0, lambda s: s % NZ * NX + (s // NZ - x) % NX),
    ):
        rows = left.shape[1]
        found = swap_far(partial_sums(left, order_of(theirs), weights))
        hidden = partial_sums(left, order_of(ours), weights, found)
        hidden = hidden.reshape(4, 4, 1, rows, hidden_here)
        parts = (hidden[0], swap_core(hidden[1]), swap_near(hidden[2]), swap_both(hidden[3]))
        for which, value in zip(quarters, parts, strict=True):
            mlp_hidden = lax.dynamic_update_slice(mlp_hidden, value, (0, which, first, 0))
    mlp_hidden = mlp_hidden.reshape(4 * tok_rows, hidden_here)
    return (mlp_hidden, kv_cache, residual_out)


def solution(mesh):
    in_specs = (
        P("dp", "mp"),
        P("dp", "mp"),
        P(None, "dp", "mp"),
        P("dp"),
        P(),
        P("dp"),
        P("dp", "mp"),
        P("mp"),
        P("mp", None, "dp"),
    )
    out_specs = (P("mp", "dp"), P("dp", None, None, "mp"), P("dp", "mp"))
    return jax.shard_map(shards, mesh=mesh, in_specs=in_specs, out_specs=out_specs, check_vma=False)
```

```python
import functools

import jax
import jax.numpy as jnp
from jax import lax
from jax.experimental import pallas as pl
from jax.experimental.pallas import tpu as pltpu
from jax.sharding import PartitionSpec as P

D = 5120
HD = 128
EPS = 1e-06
NX, NZ, NY = 4, 8, 4
ROWS_A = 32
BLOCKS = 8

BF16 = jnp.bfloat16
F32 = jnp.float32


def send_x(a, step):
    return lax.ppermute(a, "dp", [(d, (d + NZ * step) % (NX * NZ)) for d in range(NX * NZ)])


def send_z(a, step):
    return lax.ppermute(
        a, "dp", [(d, d // NZ * NZ + (d % NZ + step) % NZ) for d in range(NX * NZ)]
    )


def send_y(a, step):
    return lax.ppermute(a, "mp", [(m, (m + 2 * step) % (2 * NY)) for m in range(2 * NY)])


def swap_core(a):
    return lax.ppermute(a, "mp", [(m, m ^ 1) for m in range(2 * NY)])


def near_chip(y, core):
    return jnp.where(core == 0, y ^ 1, NY - 1 - y)


def far_chip(y, core):
    return jnp.where(core == 0, NY - 1 - y, y ^ 1)


def part_of(y, core):
    return jnp.where(core == 0, (y == 1) | (y == 2), y >= 2).astype(jnp.int32)


def swap_near(a):
    return lax.ppermute(
        a, "mp", [(m, m ^ 2 if m % 2 == 0 else 2 * NY - m) for m in range(2 * NY)]
    )


def swap_far(a):
    return lax.ppermute(
        a, "mp", [(m, 2 * NY - 2 - m if m % 2 == 0 else m ^ 2) for m in range(2 * NY)]
    )


def swap_both(a):
    return lax.ppermute(
        a, "mp", [(m, (m ^ 2) + 1 if m % 2 == 0 else 2 * NY - 1 - m) for m in range(2 * NY)]
    )


def gather_x(a):
    half = a.shape[0] // 2
    up, down = send_x(a, 1), send_x(a, -1)
    far = (send_x(up[:half], 1), send_x(down[half:], -1))
    return [(a,), (down,), far, (up,)]


def offload_z(a):
    groups = [[i * NZ + k for k in range(NZ)] for i in range(NX)]
    return lax.all_gather(a, "dp", axis=0, tiled=True, axis_index_groups=groups)


def gather_heads(a):
    half = a.shape[0] // 2
    up, down = send_y(a, 1), send_y(a, -1)
    mine = jnp.concatenate([a, down, send_y(up[:half], 1), send_y(down[half:], -1), up], axis=0)
    return jnp.concatenate([mine, swap_core(mine)], axis=0)


def gather_dp(a, b, later=None):
    half_a, half_b = a.shape[0] // 2, b.shape[0] // 2
    up_x, down_x, up_z, down_z = lax.optimization_barrier(
        (send_x(a, 1), send_x(a, -1), send_z(b, 1), send_z(b, -1))
    )
    far_x = (send_x(up_x[:half_a], 1), send_x(down_x[half_a:], -1))
    far_x, up_2, down_2 = lax.optimization_barrier((far_x, send_z(up_z, 1), send_z(down_z, -1)))
    ring_a = jnp.concatenate([a, down_x, *far_x, up_x], axis=0)
    found_a = offload_z(ring_a).reshape(NX * NZ, *a.shape)
    up_3, down_3 = send_z(up_2, 1), send_z(down_2, -1)
    far_z = (send_z(up_3[:half_b], 1), send_z(down_3[half_b:], -1))
    ring_b = [b, down_z, down_2, down_3, *far_z, up_3, up_2, up_z]
    ring_b = jnp.concatenate(ring_b, axis=0).reshape(NZ, *b.shape)
    ring_b, later = lax.optimization_barrier((ring_b, later))
    found_b = jnp.concatenate([p for part in gather_x(ring_b) for p in part], axis=0)
    return found_a, found_b, later


def attend(queries_in, key_values, request_ids):
    tok_rows = queries_in.shape[0]
    q_heads = queries_in.shape[1] // HD
    kv_heads = key_values.shape[2] // HD
    group = q_heads // kv_heads
    queries = queries_in.reshape(tok_rows, kv_heads, group, HD)
    keys = key_values[0].reshape(tok_rows, kv_heads, HD)
    values = key_values[1].reshape(tok_rows, kv_heads, HD)
    scores = jnp.einsum(
        "qhgd,khd->hgqk", queries, keys, preferred_element_type=jnp.float32
    ) * HD ** (-0.5)
    places = jnp.arange(tok_rows, dtype=jnp.int32)
    allowed = (request_ids[:, None] == request_ids[None, :]) & (places[None, :] <= places[:, None])
    scores = jnp.where(allowed, scores, -1e30)
    row_max = jnp.max(scores, axis=-1, keepdims=True)
    lifted = jnp.exp(scores - row_max)
    weights = (lifted / jnp.sum(lifted, axis=-1, keepdims=True)).astype(jnp.bfloat16)
    mixed = jnp.einsum("hgqk,khd->hgdq", weights, values, preferred_element_type=jnp.float32)
    return mixed.astype(jnp.bfloat16).reshape(q_heads * HD, tok_rows)


def product(place, attended, piece, plan, first, count):
    x, y, z, core = place[0], place[1], place[2], place[3]
    n, depth, width = piece.shape
    heads = attended.shape[0] // (2 * NY)
    per_device = heads // count
    total = None
    for low in range(0, n, BLOCKS):
        parts = []
        for i in range(low, low + BLOCKS):
            dx, z_of = plan(i, z)
            owner = lax.rem(x + dx, NX) * NZ + z_of
            m = owner // per_device
            where = jnp.bitwise_xor(lax.rem(m, 2), core) * NY + lax.rem(m // 2 - y + NY, NY)
            start = where * heads + lax.rem(owner, per_device) * count + first
            parts.append(attended[pl.ds(pl.multiple_of(start, 16), depth), :])
        left = jnp.concatenate(parts, axis=0)
        right = piece[low : low + BLOCKS].reshape(BLOCKS * depth, width)
        term = lax.dot_general(left, right, (((0,), (0,)), ((), ())), preferred_element_type=F32)
        total = term if total is None else total + term
    return total


def project_b_kernel(first, count, place, attended, residual, piece, out):
    def plan(i, z):
        return i // NZ, lax.rem(z + i % NZ, NZ)

    out[...] = residual[...].astype(F32) + product(place, attended, piece, plan, first, count)


def project_b(place, attended, residual, piece, first, count):
    vmem = pl.BlockSpec(memory_space=pltpu.VMEM)
    return pl.pallas_call(
        functools.partial(project_b_kernel, first, count),
        out_shape=jax.ShapeDtypeStruct(residual.shape, F32),
        in_specs=[pl.BlockSpec(memory_space=pltpu.SMEM)] + [vmem] * 3,
        out_specs=vmem,
        compiler_params=pltpu.CompilerParams(vmem_limit_bytes=40 * 2**20),
        name="project_b",
    )(place, attended, residual, piece)


def project_a_kernel(count, place, attended, so_far, gain, piece, resid_out, keep, send, squares):
    def plan(i, z):
        return i % NX, i // NX

    rows = so_far.shape[0]
    total = so_far[...] + product(place, attended, piece, plan, 0, count)
    resid_out[...] = total.astype(BF16)
    squares[...] = lax.dot_general(
        jnp.ones((8, total.shape[1]), F32),
        total * total,
        (((1,), (1,)), ((), ())),
        precision=lax.Precision.HIGHEST,
        preferred_element_type=F32,
    )
    scaled = total * gain[...]
    half = rows // 2
    first_half, second_half = scaled[:half], scaled[half:]
    is_first = place[3] == 0

    @pl.when(is_first)
    def _():
        keep[...] = first_half
        send[...] = second_half

    @pl.when(jnp.logical_not(is_first))
    def _():
        keep[...] = second_half
        send[...] = first_half


def project_a(place, attended, so_far, gain, piece, count):
    rows, width = so_far.shape
    vmem = pl.BlockSpec(memory_space=pltpu.VMEM)
    return pl.pallas_call(
        functools.partial(project_a_kernel, count),
        out_shape=(
            jax.ShapeDtypeStruct((rows, width), BF16),
            jax.ShapeDtypeStruct((rows // 2, width), F32),
            jax.ShapeDtypeStruct((rows // 2, width), F32),
            jax.ShapeDtypeStruct((8, rows), F32),
        ),
        in_specs=[pl.BlockSpec(memory_space=pltpu.SMEM)] + [vmem] * 4,
        out_specs=(vmem,) * 4,
        compiler_params=pltpu.CompilerParams(vmem_limit_bytes=40 * 2**20),
        name="project_a",
    )(place, attended, so_far, gain, piece)


def partial_kernel(n_add, order, left, *refs):
    weights, addends, (out, blocks, arrived) = refs[:2], refs[2 : 2 + n_add], refs[2 + n_add :]
    rows, depth = left.shape[1], weights[0].shape[0]
    count = blocks.shape[0] // rows

    def fetch(i):
        place = pl.ds(pl.multiple_of(i * rows, rows), rows)
        return pltpu.make_async_copy(left.at[order[i]], blocks.at[place], arrived.at[i])

    for i in range(count):
        fetch(i).start()

    def step(n, carry):
        for i in range(BLOCKS):
            fetch(n * BLOCKS + i).wait()
        span = pl.ds(pl.multiple_of(n * BLOCKS * rows, BLOCKS * rows), BLOCKS * rows)
        total = jnp.dot(blocks[span, :depth], weights[0][...], preferred_element_type=F32)
        total += jnp.dot(blocks[span, depth:], weights[1][...], preferred_element_type=F32)
        for addend in addends:
            total += addend[span, :].astype(F32)
        if n_add:
            half = total.shape[1] // 2
            gate, up = total[:, :half], total[:, half:]
            total = gate / (1.0 + jnp.exp(-gate)) * up
        out[span, :] = total.astype(BF16)
        return carry

    lax.fori_loop(0, count // BLOCKS, step, 0)


def partial_sums(left, order, weights, addend=None):
    rows, depth = left.shape[1:]
    width = weights[0].shape[1]
    count = order.shape[0]
    n_add = 0 if addend is None else 1
    out_width = width // 2 if n_add else width
    vmem = pl.BlockSpec(memory_space=pltpu.VMEM)
    return pl.pallas_call(
        functools.partial(partial_kernel, n_add),
        out_shape=jax.ShapeDtypeStruct((count * rows, out_width), BF16),
        in_specs=[
            pl.BlockSpec(memory_space=pltpu.SMEM),
            pl.BlockSpec(memory_space=pltpu.HBM),
            *[vmem] * (2 + n_add),
        ],
        out_specs=vmem,
        scratch_shapes=[
            pltpu.VMEM((count * rows, depth), BF16),
            pltpu.SemaphoreType.DMA((count,)),
        ],
        compiler_params=pltpu.CompilerParams(vmem_limit_bytes=46 * 2**20),
        name="last_partials" if n_add else "partials",
    )(order, left, *weights, *[addend] * n_add)


def shards(
    residual_in,
    queries_in,
    key_values,
    request_ids,
    deal_order,
    page_table,
    out_proj,
    norm_gain,
    gate_up,
):
    tok_rows, local_width = residual_in.shape
    dp_index, mp_index = lax.axis_index("dp"), lax.axis_index("mp")
    x, z = dp_index // NZ, dp_index % NZ
    y, core = mp_index // 2, mp_index % 2
    hidden_here = gate_up.shape[2]

    count = out_proj.shape[0]
    first_b = count // 2
    attended = attend(queries_in, key_values, request_ids)
    proj_a, proj_b, attended = gather_dp(out_proj[:first_b], out_proj[first_b:], attended)
    all_heads = gather_heads(attended)

    flat_weights = gate_up.reshape(local_width, 2 * hidden_here)
    chip_weights = jnp.concatenate([flat_weights, swap_core(flat_weights)], axis=0)
    weights = (chip_weights, swap_near(chip_weights))

    pages_here = page_table.shape[0]
    page_rows = tok_rows // pages_here
    channels = key_values.shape[2]
    pages = key_values.reshape(2, pages_here, page_rows, channels).transpose(1, 0, 2, 3)
    kv_cache = jnp.zeros_like(pages).at[page_table % pages_here].set(pages)

    place = jnp.stack([x, y, z, core]).astype(jnp.int32)
    so_far = project_b(place, all_heads, residual_in, proj_b, first_b, count)
    gain = norm_gain.astype(F32).reshape(1, local_width)
    so_far, weights = lax.optimization_barrier((so_far, weights))
    residual_out, keep, send, squares = project_a(place, all_heads, so_far, gain, proj_a, count)
    squares = squares + swap_core(squares)
    squares = squares + send_y(squares, 1) + send_y(squares, -1) + send_y(squares, 2)
    quarter = tok_rows // 4
    part = part_of(y, core)
    chip = jnp.concatenate([keep, swap_core(send)], axis=1)
    mine = lax.dynamic_slice_in_dim(chip, part * quarter, quarter, 0)
    other = lax.dynamic_slice_in_dim(chip, (1 - part) * quarter, quarter, 0)
    mine = jnp.concatenate([mine, swap_near(other)], axis=1)
    own_squares = lax.dynamic_slice_in_dim(squares[0], (2 * core + part) * quarter, quarter, 0)
    mine = (mine * lax.rsqrt(own_squares / D + EPS)[:, None]).astype(BF16)

    nblocks = deal_order.shape[0]
    per_chip = nblocks // NY

    def blocks_of(first_chip):
        places = [
            (chip * 2 + which) * 4 + jnp.arange(4, dtype=jnp.int32)
            for chip in (first_chip, near_chip(first_chip, core))
            for which in (core, 1 - core)
        ]
        return jnp.take(deal_order, jnp.concatenate(places), mode="clip")

    theirs, ours = blocks_of(far_chip(y, core)), blocks_of(y)
    left_a, left_b, _ = gather_dp(mine[:ROWS_A], mine[ROWS_A:])

    other_part = part_of(y, 1 - core)
    quarters = (
        2 * core + part,
        2 * (1 - core) + other_part,
        2 * core + 1 - part,
        2 * (1 - core) + 1 - other_part,
    )
    mlp_hidden = jnp.zeros((4, 4, quarter, hidden_here), BF16)
    for left, first, order_of in (
        (left_b, ROWS_A, lambda s: (s // NZ - x) % NX * NZ + (s % NZ - z) % NZ),
        (left_a, 0, lambda s: s % NZ * NX + (s // NZ - x) % NX),
    ):
        rows = left.shape[1]
        found = swap_far(partial_sums(left, order_of(theirs), weights))
        hidden = partial_sums(left, order_of(ours), weights, found)
        hidden = hidden.reshape(4, 4, 1, rows, hidden_here)
        parts = (hidden[0], swap_core(hidden[1]), swap_near(hidden[2]), swap_both(hidden[3]))
        for which, value in zip(quarters, parts, strict=True):
            mlp_hidden = lax.dynamic_update_slice(mlp_hidden, value, (0, which, first, 0))
    mlp_hidden = mlp_hidden.reshape(4 * tok_rows, hidden_here)
    return (mlp_hidden, kv_cache, residual_out)


def solution(mesh):
    in_specs = (
        P("dp", "mp"),
        P("dp", "mp"),
        P(None, "dp", "mp"),
        P("dp"),
        P(),
        P("dp"),
        P("dp", "mp"),
        P("mp"),
        P("mp", None, "dp"),
    )
    out_specs = (P("mp", "dp"), P("dp", None, None, "mp"), P("dp", "mp"))
    return jax.shard_map(shards, mesh=mesh, in_specs=in_specs, out_specs=out_specs, check_vma=False)
```

```python
import functools

import jax
import jax.numpy as jnp
from jax import lax
from jax.experimental import pallas as pl
from jax.experimental.pallas import tpu as pltpu
from jax.sharding import PartitionSpec as P

D = 5120
HD = 128
EPS = 1e-06
NX, NZ, NY = 4, 8, 4
ROWS_A = 32
BLOCKS = 8

BF16 = jnp.bfloat16
F32 = jnp.float32


def send_x(a, step):
    return lax.ppermute(a, "dp", [(d, (d + NZ * step) % (NX * NZ)) for d in range(NX * NZ)])


def send_z(a, step):
    return lax.ppermute(
        a, "dp", [(d, d // NZ * NZ + (d % NZ + step) % NZ) for d in range(NX * NZ)]
    )


def send_y(a, step):
    return lax.ppermute(a, "mp", [(m, (m + 2 * step) % (2 * NY)) for m in range(2 * NY)])


def swap_core(a):
    return lax.ppermute(a, "mp", [(m, m ^ 1) for m in range(2 * NY)])


def near_chip(y, core):
    return jnp.where(core == 0, y ^ 1, NY - 1 - y)


def far_chip(y, core):
    return jnp.where(core == 0, NY - 1 - y, y ^ 1)


def part_of(y, core):
    return jnp.where(core == 0, (y == 1) | (y == 2), y >= 2).astype(jnp.int32)


def swap_near(a):
    return lax.ppermute(
        a, "mp", [(m, m ^ 2 if m % 2 == 0 else 2 * NY - m) for m in range(2 * NY)]
    )


def swap_far(a):
    return lax.ppermute(
        a, "mp", [(m, 2 * NY - 2 - m if m % 2 == 0 else m ^ 2) for m in range(2 * NY)]
    )


def swap_both(a):
    return lax.ppermute(
        a, "mp", [(m, (m ^ 2) + 1 if m % 2 == 0 else 2 * NY - 1 - m) for m in range(2 * NY)]
    )


def exchange(hidden):
    return (hidden[0], swap_core(hidden[1]), swap_near(hidden[2]), swap_both(hidden[3]))


def gather_x(a):
    half = a.shape[0] // 2
    up, down = send_x(a, 1), send_x(a, -1)
    far = (send_x(up[:half], 1), send_x(down[half:], -1))
    return [(a,), (down,), far, (up,)]


def offload_z(a):
    groups = [[i * NZ + k for k in range(NZ)] for i in range(NX)]
    return lax.all_gather(a, "dp", axis=0, tiled=True, axis_index_groups=groups)


def gather_z(a):
    half = a.shape[0] // 2
    ups, downs = [a], [a]
    for _ in range(NZ // 2 - 1):
        ups.append(send_z(ups[-1], 1))
        downs.append(send_z(downs[-1], -1))
    far = (send_z(ups[-1][:half], 1), send_z(downs[-1][half:], -1))
    return [(a,)] + [(d,) for d in downs[1:]] + [far] + [(u,) for u in ups[:0:-1]]


def gather_xz(a):
    ring = jnp.concatenate([piece for part in gather_x(a) for piece in part], axis=0)
    ring = ring.reshape(NX, a.shape[0], a.shape[1])
    out = []
    for z, part in enumerate(gather_z(ring)):
        base = 0
        for piece in part:
            out.append((base, z, piece))
            base += piece.shape[0]
    return out


def gather_zx(b):
    ring = jnp.concatenate([piece for part in gather_z(b) for piece in part], axis=0)
    ring = ring.reshape(NZ, b.shape[0], b.shape[1])
    out = []
    for x, part in enumerate(gather_x(ring)):
        base = 0
        for piece in part:
            out.append((x, base, piece))
            base += piece.shape[0]
    return out


def gather_dp(a, b):
    half_a, half_b = a.shape[0] // 2, b.shape[0] // 2
    up_x, down_x, up_z, down_z = lax.optimization_barrier(
        (send_x(a, 1), send_x(a, -1), send_z(b, 1), send_z(b, -1))
    )
    far_x = (send_x(up_x[:half_a], 1), send_x(down_x[half_a:], -1))
    far_x, up_2, down_2 = lax.optimization_barrier((far_x, send_z(up_z, 1), send_z(down_z, -1)))
    ring_a = jnp.concatenate([a, down_x, *far_x, up_x], axis=0)
    found_a = offload_z(ring_a).reshape(NX * NZ, *a.shape)
    up_3, down_3 = send_z(up_2, 1), send_z(down_2, -1)
    far_z = (send_z(up_3[:half_b], 1), send_z(down_3[half_b:], -1))
    ring_b = [b, down_z, down_2, down_3, *far_z, up_3, up_2, up_z]
    ring_b = jnp.concatenate(ring_b, axis=0).reshape(NZ, *b.shape)
    found_b = jnp.concatenate([p for part in gather_x(ring_b) for p in part], axis=0)
    return found_a, found_b


def attend(queries_in, key_values, request_ids):
    tok_rows = queries_in.shape[0]
    q_heads = queries_in.shape[1] // HD
    kv_heads = key_values.shape[2] // HD
    group = q_heads // kv_heads
    queries = queries_in.reshape(tok_rows, kv_heads, group, HD)
    keys = key_values[0].reshape(tok_rows, kv_heads, HD)
    values = key_values[1].reshape(tok_rows, kv_heads, HD)
    scores = jnp.einsum(
        "qhgd,khd->hgqk", queries, keys, preferred_element_type=jnp.float32
    ) * HD ** (-0.5)
    places = jnp.arange(tok_rows, dtype=jnp.int32)
    allowed = (request_ids[:, None] == request_ids[None, :]) & (places[None, :] <= places[:, None])
    scores = jnp.where(allowed, scores, -1e30)
    row_max = jnp.max(scores, axis=-1, keepdims=True)
    lifted = jnp.exp(scores - row_max)
    weights = (lifted / jnp.sum(lifted, axis=-1, keepdims=True)).astype(jnp.bfloat16)
    mixed = jnp.einsum("hgqk,khd->hgdq", weights, values, preferred_element_type=jnp.float32)
    return mixed.astype(jnp.bfloat16).reshape(q_heads * HD, tok_rows)


def project_kernel(plan, place, attended, residual, gain, *refs):
    pieces, (resid_out, keep, send, squares) = refs[: len(plan)], refs[len(plan) :]
    x, z, core = place[0], place[1], place[2]
    rows = residual.shape[0]
    total = residual[...].astype(F32)
    for (kind, x0, z0, first, count), piece in zip(plan, pieces, strict=True):
        n, depth, width = piece.shape
        parts = []
        for i in range(n):
            dx, dz = (x0 + i, z0) if kind == "xz" else (x0, z0 + i)
            owner = lax.rem(x + dx, NX) * NZ + lax.rem(z + dz, NZ)
            start = pl.multiple_of(owner * count + first, 16)
            parts.append(attended[pl.ds(start, depth), :])
        left = jnp.concatenate(parts, axis=0)
        right = piece[...].reshape(n * depth, width)
        total += lax.dot_general(left, right, (((0,), (0,)), ((), ())), preferred_element_type=F32)
    resid_out[...] = total.astype(BF16)
    squares[...] = lax.dot_general(
        jnp.ones((8, total.shape[1]), F32),
        total * total,
        (((1,), (1,)), ((), ())),
        precision=lax.Precision.HIGHEST,
        preferred_element_type=F32,
    )
    scaled = total * gain[...]
    half = rows // 2
    first_half, second_half = scaled[:half], scaled[half:]
    is_first = core == 0

    @pl.when(is_first)
    def _():
        keep[...] = first_half
        send[...] = second_half

    @pl.when(jnp.logical_not(is_first))
    def _():
        keep[...] = second_half
        send[...] = first_half


def project(place, attended, residual, gain, pieces, plan):
    rows, width = residual.shape
    vmem = pl.BlockSpec(memory_space=pltpu.VMEM)
    return pl.pallas_call(
        functools.partial(project_kernel, plan),
        out_shape=(
            jax.ShapeDtypeStruct((rows, width), BF16),
            jax.ShapeDtypeStruct((rows // 2, width), F32),
            jax.ShapeDtypeStruct((rows // 2, width), F32),
            jax.ShapeDtypeStruct((8, rows), F32),
        ),
        in_specs=[pl.BlockSpec(memory_space=pltpu.SMEM)] + [vmem] * (3 + len(pieces)),
        out_specs=(vmem,) * 4,
        name="project",
    )(place, attended, residual, gain, *pieces)


def partial_kernel(n_add, order, left, *refs):
    near, far, addends = refs[0], refs[1], refs[2 : 2 + n_add]
    out, blocks, arrived, far_here, far_arrived = refs[2 + n_add :]
    rows, depth = left.shape[1], near.shape[0]
    count = blocks.shape[0] // rows

    def fetch(i):
        place = pl.ds(pl.multiple_of(i * rows, rows), rows)
        return pltpu.make_async_copy(left.at[order[i]], blocks.at[place], arrived.at[i])

    fetch_far = pltpu.make_async_copy(far, far_here, far_arrived)
    for i in range(count):
        if i == BLOCKS:
            fetch_far.start()
        fetch(i).start()

    def step(n, carry):
        for i in range(BLOCKS):
            fetch(n * BLOCKS + i).wait()
        span = pl.ds(pl.multiple_of(n * BLOCKS * rows, BLOCKS * rows), BLOCKS * rows)
        total = jnp.dot(blocks[span, :depth], near[...], preferred_element_type=F32)

        @pl.when(n == 0)
        def _():
            fetch_far.wait()

        total += jnp.dot(blocks[span, depth:], far_here[...], preferred_element_type=F32)
        for addend in addends:
            total += addend[span, :].astype(F32)
        if n_add:
            half = total.shape[1] // 2
            gate, up = total[:, :half], total[:, half:]
            total = gate / (1.0 + jnp.exp(-gate)) * up
        out[span, :] = total.astype(BF16)
        return carry

    lax.fori_loop(0, count // BLOCKS, step, 0)


def partial_sums(left, order, weights, addend=None):
    rows, depth = left.shape[1:]
    width = weights[0].shape[1]
    count = order.shape[0]
    n_add = 0 if addend is None else 1
    out_width = width // 2 if n_add else width
    vmem = pl.BlockSpec(memory_space=pltpu.VMEM)
    return pl.pallas_call(
        functools.partial(partial_kernel, n_add),
        out_shape=jax.ShapeDtypeStruct((count * rows, out_width), BF16),
        in_specs=[
            pl.BlockSpec(memory_space=pltpu.SMEM),
            pl.BlockSpec(memory_space=pltpu.HBM),
            vmem,
            pl.BlockSpec(memory_space=pltpu.HBM),
            *[vmem] * n_add,
        ],
        out_specs=vmem,
        scratch_shapes=[
            pltpu.VMEM((count * rows, depth), BF16),
            pltpu.SemaphoreType.DMA((count,)),
            pltpu.VMEM(weights[1].shape, BF16),
            pltpu.SemaphoreType.DMA,
        ],
        compiler_params=pltpu.CompilerParams(vmem_limit_bytes=46 * 2**20),
        name="last_partials" if n_add else "partials",
    )(order, left, *weights, *[addend] * n_add)


def shards(
    residual_in,
    queries_in,
    key_values,
    request_ids,
    deal_order,
    page_table,
    out_proj,
    norm_gain,
    gate_up,
):
    tok_rows, local_width = residual_in.shape
    dp_index, mp_index = lax.axis_index("dp"), lax.axis_index("mp")
    x, z = dp_index // NZ, dp_index % NZ
    y, core = mp_index // 2, mp_index % 2
    hidden_here = gate_up.shape[2]

    proj_rows = out_proj.shape[0]
    proj_a = proj_rows // 2
    found_a = gather_xz(out_proj[:proj_a])
    found_b = gather_zx(out_proj[proj_a:])
    plan = [("xz", x0, z0, 0, proj_rows) for x0, z0, _ in found_a]
    plan += [("zx", x0, z0, proj_a, proj_rows) for x0, z0, _ in found_b]
    pieces = [piece for _, _, piece in found_a + found_b]

    attended = attend(queries_in, key_values, request_ids)
    all_heads = lax.all_gather(attended, "mp", axis=0, tiled=True)

    flat_weights = gate_up.reshape(local_width, 2 * hidden_here)
    chip_weights = jnp.concatenate([flat_weights, swap_core(flat_weights)], axis=0)
    weights = (chip_weights, swap_near(chip_weights))

    pages_here = page_table.shape[0]
    page_rows = tok_rows // pages_here
    channels = key_values.shape[2]
    pages = key_values.reshape(2, pages_here, page_rows, channels).transpose(1, 0, 2, 3)
    kv_cache = jnp.zeros_like(pages).at[page_table % pages_here].set(pages)

    place = jnp.stack([x, z, core]).astype(jnp.int32)
    place, weights = lax.optimization_barrier((place, weights))
    residual_out, keep, send, squares = project(
        place,
        all_heads,
        residual_in,
        norm_gain.astype(F32).reshape(1, local_width),
        pieces,
        plan,
    )
    received, other_squares = lax.optimization_barrier((swap_core(send), swap_core(squares)))
    squares = squares + other_squares
    squares = squares + send_y(squares, 1) + send_y(squares, -1) + send_y(squares, 2)
    quarter = tok_rows // 4
    part = part_of(y, core)
    chip = jnp.concatenate([keep, received], axis=1)
    mine = lax.dynamic_slice_in_dim(chip, part * quarter, quarter, 0)
    other = lax.dynamic_slice_in_dim(chip, (1 - part) * quarter, quarter, 0)
    mine = jnp.concatenate([mine, swap_near(other)], axis=1)
    own_squares = lax.dynamic_slice_in_dim(squares[0], (2 * core + part) * quarter, quarter, 0)
    mine = (mine * lax.rsqrt(own_squares / D + EPS)[:, None]).astype(BF16)

    nblocks = deal_order.shape[0]
    per_chip = nblocks // NY

    def blocks_of(first_chip):
        places = [
            (chip * 2 + which) * 4 + jnp.arange(4, dtype=jnp.int32)
            for chip in (first_chip, near_chip(first_chip, core))
            for which in (core, 1 - core)
        ]
        return jnp.take(deal_order, jnp.concatenate(places), mode="clip")

    theirs, ours = blocks_of(far_chip(y, core)), blocks_of(y)
    left_a, left_b = gather_dp(mine[:ROWS_A], mine[ROWS_A:])

    other_part = part_of(y, 1 - core)
    quarters = (
        2 * core + part,
        2 * (1 - core) + other_part,
        2 * core + 1 - part,
        2 * (1 - core) + 1 - other_part,
    )
    order_b = lambda s: (s // NZ - x) % NX * NZ + (s % NZ - z) % NZ
    order_a = lambda s: s % NZ * NX + (s // NZ - x) % NX
    rows_b = quarter - ROWS_A
    found_b = swap_far(partial_sums(left_b, order_b(theirs), weights))
    found_a = swap_far(partial_sums(left_a, order_a(theirs), weights))
    hidden_b = partial_sums(left_b, order_b(ours), weights, found_b)
    hidden_b = hidden_b.reshape(4, 4, 1, rows_b, hidden_here)
    parts_b = exchange(hidden_b)
    hidden_a = partial_sums(left_a, order_a(ours), weights, found_a)
    parts_b, hidden_a = lax.optimization_barrier((parts_b, hidden_a))
    parts_a = exchange(hidden_a.reshape(4, 4, 1, ROWS_A, hidden_here))
    mlp_hidden = jnp.zeros((4, 4, quarter, hidden_here), BF16)
    for parts, first in ((parts_b, ROWS_A), (parts_a, 0)):
        for which, value in zip(quarters, parts, strict=True):
            mlp_hidden = lax.dynamic_update_slice(mlp_hidden, value, (0, which, first, 0))
    mlp_hidden = mlp_hidden.reshape(4 * tok_rows, hidden_here)
    return (mlp_hidden, kv_cache, residual_out)


def solution(mesh):
    in_specs = (
        P("dp", "mp"),
        P("dp", "mp"),
        P(None, "dp", "mp"),
        P("dp"),
        P(),
        P("dp"),
        P("dp", "mp"),
        P("mp"),
        P("mp", None, "dp"),
    )
    out_specs = (P("mp", "dp"), P("dp", None, None, "mp"), P("dp", "mp"))
    return jax.shard_map(shards, mesh=mesh, in_specs=in_specs, out_specs=out_specs, check_vma=False)
```

```python
import functools

import jax
import jax.numpy as jnp
from jax import lax
from jax.experimental import pallas as pl
from jax.experimental.pallas import tpu as pltpu
from jax.sharding import PartitionSpec as P

D = 5120
HD = 128
EPS = 1e-06
NX, NZ, NY = 4, 8, 4
ROWS_A = 32
BLOCKS = 8

BF16 = jnp.bfloat16
F32 = jnp.float32


def send_x(a, step):
    return lax.ppermute(a, "dp", [(d, (d + NZ * step) % (NX * NZ)) for d in range(NX * NZ)])


def send_z(a, step):
    return lax.ppermute(
        a, "dp", [(d, d // NZ * NZ + (d % NZ + step) % NZ) for d in range(NX * NZ)]
    )


def send_y(a, step):
    return lax.ppermute(a, "mp", [(m, (m + 2 * step) % (2 * NY)) for m in range(2 * NY)])


def swap_core(a):
    return lax.ppermute(a, "mp", [(m, m ^ 1) for m in range(2 * NY)])


def near_chip(y, core):
    return jnp.where(core == 0, y ^ 1, NY - 1 - y)


def far_chip(y, core):
    return jnp.where(core == 0, NY - 1 - y, y ^ 1)


def part_of(y, core):
    return jnp.where(core == 0, (y == 1) | (y == 2), y >= 2).astype(jnp.int32)


def swap_near(a):
    return lax.ppermute(
        a, "mp", [(m, m ^ 2 if m % 2 == 0 else 2 * NY - m) for m in range(2 * NY)]
    )


def swap_far(a):
    return lax.ppermute(
        a, "mp", [(m, 2 * NY - 2 - m if m % 2 == 0 else m ^ 2) for m in range(2 * NY)]
    )


def swap_both(a):
    return lax.ppermute(
        a, "mp", [(m, (m ^ 2) + 1 if m % 2 == 0 else 2 * NY - 1 - m) for m in range(2 * NY)]
    )


def exchange(hidden):
    return (hidden[0], swap_core(hidden[1]), swap_near(hidden[2]), swap_both(hidden[3]))


def gather_x(a):
    half = a.shape[0] // 2
    up, down = send_x(a, 1), send_x(a, -1)
    far = (send_x(up[:half], 1), send_x(down[half:], -1))
    return [(a,), (down,), far, (up,)]


def offload_z(a):
    groups = [[i * NZ + k for k in range(NZ)] for i in range(NX)]
    return lax.all_gather(a, "dp", axis=0, tiled=True, axis_index_groups=groups)


def gather_z(a):
    half = a.shape[0] // 2
    ups, downs = [a], [a]
    for _ in range(NZ // 2 - 1):
        ups.append(send_z(ups[-1], 1))
        downs.append(send_z(downs[-1], -1))
    far = (send_z(ups[-1][:half], 1), send_z(downs[-1][half:], -1))
    return [(a,)] + [(d,) for d in downs[1:]] + [far] + [(u,) for u in ups[:0:-1]]


def gather_xz(a):
    ring = jnp.concatenate([piece for part in gather_x(a) for piece in part], axis=0)
    ring = ring.reshape(NX, a.shape[0], a.shape[1])
    out = []
    for z, part in enumerate(gather_z(ring)):
        base = 0
        for piece in part:
            out.append((base, z, piece))
            base += piece.shape[0]
    return out


def gather_zx(b):
    ring = jnp.concatenate([piece for part in gather_z(b) for piece in part], axis=0)
    ring = ring.reshape(NZ, b.shape[0], b.shape[1])
    out = []
    for x, part in enumerate(gather_x(ring)):
        base = 0
        for piece in part:
            out.append((x, base, piece))
            base += piece.shape[0]
    return out


def gather_dp(a, b):
    half_a, half_b = a.shape[0] // 2, b.shape[0] // 2
    up_x, down_x, up_z, down_z = lax.optimization_barrier(
        (send_x(a, 1), send_x(a, -1), send_z(b, 1), send_z(b, -1))
    )
    far_x = (send_x(up_x[:half_a], 1), send_x(down_x[half_a:], -1))
    far_x, up_2, down_2 = lax.optimization_barrier((far_x, send_z(up_z, 1), send_z(down_z, -1)))
    ring_a = jnp.concatenate([a, down_x, *far_x, up_x], axis=0)
    found_a = offload_z(ring_a).reshape(NX * NZ, *a.shape)
    up_3, down_3 = send_z(up_2, 1), send_z(down_2, -1)
    far_z = (send_z(up_3[:half_b], 1), send_z(down_3[half_b:], -1))
    ring_b = [b, down_z, down_2, down_3, *far_z, up_3, up_2, up_z]
    ring_b = jnp.concatenate(ring_b, axis=0).reshape(NZ, *b.shape)
    found_b = jnp.concatenate([p for part in gather_x(ring_b) for p in part], axis=0)
    return found_a, found_b


def attend(queries_in, key_values, request_ids):
    tok_rows = queries_in.shape[0]
    q_heads = queries_in.shape[1] // HD
    kv_heads = key_values.shape[2] // HD
    group = q_heads // kv_heads
    queries = queries_in.reshape(tok_rows, kv_heads, group, HD)
    keys = key_values[0].reshape(tok_rows, kv_heads, HD)
    values = key_values[1].reshape(tok_rows, kv_heads, HD)
    scores = jnp.einsum(
        "qhgd,khd->hgqk", queries, keys, preferred_element_type=jnp.float32
    ) * HD ** (-0.5)
    places = jnp.arange(tok_rows, dtype=jnp.int32)
    allowed = (request_ids[:, None] == request_ids[None, :]) & (places[None, :] <= places[:, None])
    scores = jnp.where(allowed, scores, -1e30)
    row_max = jnp.max(scores, axis=-1, keepdims=True)
    lifted = jnp.exp(scores - row_max)
    weights = (lifted / jnp.sum(lifted, axis=-1, keepdims=True)).astype(jnp.bfloat16)
    mixed = jnp.einsum("hgqk,khd->hgdq", weights, values, preferred_element_type=jnp.float32)
    return mixed.astype(jnp.bfloat16).reshape(q_heads * HD, tok_rows)


def project_kernel(plan, place, attended, residual, gain, *refs):
    pieces, (resid_out, keep, send, squares) = refs[: len(plan)], refs[len(plan) :]
    x, z, core = place[0], place[1], place[2]
    rows = residual.shape[0]
    total = residual[...].astype(F32)
    for (kind, x0, z0, first, count), piece in zip(plan, pieces, strict=True):
        n, depth, width = piece.shape
        parts = []
        for i in range(n):
            dx, dz = (x0 + i, z0) if kind == "xz" else (x0, z0 + i)
            owner = lax.rem(x + dx, NX) * NZ + lax.rem(z + dz, NZ)
            start = pl.multiple_of(owner * count + first, 16)
            parts.append(attended[pl.ds(start, depth), :])
        left = jnp.concatenate(parts, axis=0)
        right = piece[...].reshape(n * depth, width)
        total += lax.dot_general(left, right, (((0,), (0,)), ((), ())), preferred_element_type=F32)
    resid_out[...] = total.astype(BF16)
    squares[...] = lax.dot_general(
        jnp.ones((8, total.shape[1]), F32),
        total * total,
        (((1,), (1,)), ((), ())),
        precision=lax.Precision.HIGHEST,
        preferred_element_type=F32,
    )
    scaled = total * gain[...]
    half = rows // 2
    first_half, second_half = scaled[:half], scaled[half:]
    is_first = core == 0

    @pl.when(is_first)
    def _():
        keep[...] = first_half
        send[...] = second_half

    @pl.when(jnp.logical_not(is_first))
    def _():
        keep[...] = second_half
        send[...] = first_half


def project(place, attended, residual, gain, pieces, plan):
    rows, width = residual.shape
    vmem = pl.BlockSpec(memory_space=pltpu.VMEM)
    return pl.pallas_call(
        functools.partial(project_kernel, plan),
        out_shape=(
            jax.ShapeDtypeStruct((rows, width), BF16),
            jax.ShapeDtypeStruct((rows // 2, width), F32),
            jax.ShapeDtypeStruct((rows // 2, width), F32),
            jax.ShapeDtypeStruct((8, rows), F32),
        ),
        in_specs=[pl.BlockSpec(memory_space=pltpu.SMEM)] + [vmem] * (3 + len(pieces)),
        out_specs=(vmem,) * 4,
        name="project",
    )(place, attended, residual, gain, *pieces)


def partial_kernel(n_add, order, left, *refs):
    weights, addends, (out, blocks, arrived) = refs[:2], refs[2 : 2 + n_add], refs[2 + n_add :]
    rows, depth = left.shape[1], weights[0].shape[0]
    count = blocks.shape[0] // rows

    def fetch(i):
        place = pl.ds(pl.multiple_of(i * rows, rows), rows)
        return pltpu.make_async_copy(left.at[order[i]], blocks.at[place], arrived.at[i])

    for i in range(count):
        fetch(i).start()

    def step(n, carry):
        for i in range(BLOCKS):
            fetch(n * BLOCKS + i).wait()
        span = pl.ds(pl.multiple_of(n * BLOCKS * rows, BLOCKS * rows), BLOCKS * rows)
        total = jnp.dot(blocks[span, :depth], weights[0][...], preferred_element_type=F32)
        total += jnp.dot(blocks[span, depth:], weights[1][...], preferred_element_type=F32)
        for addend in addends:
            total += addend[span, :].astype(F32)
        if n_add:
            half = total.shape[1] // 2
            gate, up = total[:, :half], total[:, half:]
            total = gate / (1.0 + jnp.exp(-gate)) * up
        out[span, :] = total.astype(BF16)
        return carry

    lax.fori_loop(0, count // BLOCKS, step, 0)


def partial_sums(left, order, weights, addend=None):
    rows, depth = left.shape[1:]
    width = weights[0].shape[1]
    count = order.shape[0]
    n_add = 0 if addend is None else 1
    out_width = width // 2 if n_add else width
    vmem = pl.BlockSpec(memory_space=pltpu.VMEM)
    return pl.pallas_call(
        functools.partial(partial_kernel, n_add),
        out_shape=jax.ShapeDtypeStruct((count * rows, out_width), BF16),
        in_specs=[
            pl.BlockSpec(memory_space=pltpu.SMEM),
            pl.BlockSpec(memory_space=pltpu.HBM),
            *[vmem] * (2 + n_add),
        ],
        out_specs=vmem,
        scratch_shapes=[
            pltpu.VMEM((count * rows, depth), BF16),
            pltpu.SemaphoreType.DMA((count,)),
        ],
        compiler_params=pltpu.CompilerParams(vmem_limit_bytes=46 * 2**20),
        name="last_partials" if n_add else "partials",
    )(order, left, *weights, *[addend] * n_add)


def shards(
    residual_in,
    queries_in,
    key_values,
    request_ids,
    deal_order,
    page_table,
    out_proj,
    norm_gain,
    gate_up,
):
    tok_rows, local_width = residual_in.shape
    dp_index, mp_index = lax.axis_index("dp"), lax.axis_index("mp")
    x, z = dp_index // NZ, dp_index % NZ
    y, core = mp_index // 2, mp_index % 2
    hidden_here = gate_up.shape[2]

    proj_rows = out_proj.shape[0]
    proj_a = proj_rows // 2
    found_a = gather_xz(out_proj[:proj_a])
    found_b = gather_zx(out_proj[proj_a:])
    plan = [("xz", x0, z0, 0, proj_rows) for x0, z0, _ in found_a]
    plan += [("zx", x0, z0, proj_a, proj_rows) for x0, z0, _ in found_b]
    pieces = [piece for _, _, piece in found_a + found_b]

    attended = attend(queries_in, key_values, request_ids)
    all_heads = lax.all_gather(attended, "mp", axis=0, tiled=True)

    flat_weights = gate_up.reshape(local_width, 2 * hidden_here)
    chip_weights = jnp.concatenate([flat_weights, swap_core(flat_weights)], axis=0)
    weights = (chip_weights, swap_near(chip_weights))

    pages_here = page_table.shape[0]
    page_rows = tok_rows // pages_here
    channels = key_values.shape[2]
    pages = key_values.reshape(2, pages_here, page_rows, channels).transpose(1, 0, 2, 3)
    kv_cache = jnp.zeros_like(pages).at[page_table % pages_here].set(pages)

    place = jnp.stack([x, z, core]).astype(jnp.int32)
    place, weights = lax.optimization_barrier((place, weights))
    residual_out, keep, send, squares = project(
        place,
        all_heads,
        residual_in,
        norm_gain.astype(F32).reshape(1, local_width),
        pieces,
        plan,
    )
    received, other_squares = lax.optimization_barrier((swap_core(send), swap_core(squares)))
    squares = squares + other_squares
    squares = squares + send_y(squares, 1) + send_y(squares, -1) + send_y(squares, 2)
    quarter = tok_rows // 4
    part = part_of(y, core)
    chip = jnp.concatenate([keep, received], axis=1)
    mine = lax.dynamic_slice_in_dim(chip, part * quarter, quarter, 0)
    other = lax.dynamic_slice_in_dim(chip, (1 - part) * quarter, quarter, 0)
    mine = jnp.concatenate([mine, swap_near(other)], axis=1)
    own_squares = lax.dynamic_slice_in_dim(squares[0], (2 * core + part) * quarter, quarter, 0)
    mine = (mine * lax.rsqrt(own_squares / D + EPS)[:, None]).astype(BF16)

    nblocks = deal_order.shape[0]
    per_chip = nblocks // NY

    def blocks_of(first_chip):
        places = [
            (chip * 2 + which) * 4 + jnp.arange(4, dtype=jnp.int32)
            for chip in (first_chip, near_chip(first_chip, core))
            for which in (core, 1 - core)
        ]
        return jnp.take(deal_order, jnp.concatenate(places), mode="clip")

    theirs, ours = blocks_of(far_chip(y, core)), blocks_of(y)
    left_a, left_b = gather_dp(mine[:ROWS_A], mine[ROWS_A:])

    other_part = part_of(y, 1 - core)
    quarters = (
        2 * core + part,
        2 * (1 - core) + other_part,
        2 * core + 1 - part,
        2 * (1 - core) + 1 - other_part,
    )
    order_b = lambda s: (s // NZ - x) % NX * NZ + (s % NZ - z) % NZ
    order_a = lambda s: s % NZ * NX + (s // NZ - x) % NX
    rows_b = quarter - ROWS_A
    found_b = swap_far(partial_sums(left_b, order_b(theirs), weights))
    found_a = swap_far(partial_sums(left_a, order_a(theirs), weights))
    hidden_b = partial_sums(left_b, order_b(ours), weights, found_b)
    hidden_b = hidden_b.reshape(4, 4, 1, rows_b, hidden_here)
    parts_b = exchange(hidden_b)
    hidden_a = partial_sums(left_a, order_a(ours), weights, found_a)
    parts_b, hidden_a = lax.optimization_barrier((parts_b, hidden_a))
    parts_a = exchange(hidden_a.reshape(4, 4, 1, ROWS_A, hidden_here))
    mlp_hidden = jnp.zeros((4, 4, quarter, hidden_here), BF16)
    for parts, first in ((parts_b, ROWS_A), (parts_a, 0)):
        for which, value in zip(quarters, parts, strict=True):
            mlp_hidden = lax.dynamic_update_slice(mlp_hidden, value, (0, which, first, 0))
    mlp_hidden = mlp_hidden.reshape(4 * tok_rows, hidden_here)
    return (mlp_hidden, kv_cache, residual_out)


def solution(mesh):
    in_specs = (
        P("dp", "mp"),
        P("dp", "mp"),
        P(None, "dp", "mp"),
        P("dp"),
        P(),
        P("dp"),
        P("dp", "mp"),
        P("mp"),
        P("mp", None, "dp"),
    )
    out_specs = (P("mp", "dp"), P("dp", None, None, "mp"), P("dp", "mp"))
    return jax.shard_map(shards, mesh=mesh, in_specs=in_specs, out_specs=out_specs, check_vma=False)
```
